256 devices in a mesh: section: 8 (over z_lo, y), row: 8 (over x, core), col: 4 (over z_hi).
Axes of the slice: x: 4, y: 4, z: 8 (z_hi: 4, z_lo: 2; z = z_hi * 2 + z_lo), core: 2. Of those that a mesh axis runs over, the one named last changes fastest.
Arguments:
- x_down: bfloat16 [8, 1024, 8192], P('section', 'row', 'col'), may hold values from -30 to 30
- gain_down: float32 [8, 8192], P('section', 'col'), may hold values from 0.1 to 1.9
- wq_down: bfloat16 [8, 8192, 4096], P('section', 'col', 'row'), may hold values from -2 to 2
- wk_down: bfloat16 [8, 8192, 512], P('section', 'col', 'row'), may hold values from -1 to 1
- wv_down: bfloat16 [8, 8192, 512], P('section', 'col', 'row'), may hold values from -0.0625 to 0.0625
- wo_down: bfloat16 [8, 4096, 8192], P('section', 'row', 'col'), may hold values from -0.09375 to 0.09375
- x_up: bfloat16 [8, 1024, 8192], P('section', 'row', 'col'), may hold values from -30 to 30
- gain_up: float32 [8, 8192], P('section', 'col'), may hold values from 0.1 to 1.9
- wq_up: bfloat16 [8, 8192, 4096], P('section', 'col', 'row'), may hold values from -2 to 2
- wk_up: bfloat16 [8, 8192, 512], P('section', 'col', 'row'), may hold values from -1 to 1
- wv_up: bfloat16 [8, 8192, 512], P('section', 'col', 'row'), may hold values from -0.0625 to 0.0625
- wo_up: bfloat16 [8, 4096, 8192], P('section', 'row', 'col'), may hold values from -0.09375 to 0.09375
Outputs:
- next_down: bfloat16 [8, 1024, 8192], P('section', 'row', 'col')
- next_up: bfloat16 [8, 1024, 8192], P('section', 'row', 'col')
The draws below stay inside these ranges and needn't reach their ends.
All inputs are finite; a program needn't handle non-finite values.
Results may differ from the reference program's by a relative error of at most 0.0055.
Values may be sent and summed in bfloat16 or wider, within the bound.
A program may use at most 128 MiB of HBM per device.

```python
import math
import jax
import jax.numpy as jnp
from jax import lax

D = 8192
HEADS = 32
KV_HEADS = 4
HD = 128
TOKENS = 1024
HQ = 4096
KVW = 512
SECTIONS = 8
N_ROW = 8


def activations(key):
    noise_key, row_key, col_key = jax.random.split(key, 3)
    ramp = jnp.arange(D, dtype=jnp.float32) / D
    noise = jnp.clip(jax.random.normal(noise_key, (SECTIONS, TOKENS, D), jnp.float32), -3.0, 3.0)
    slope = 1.0 + 0.8 * ramp
    row_scale = jnp.exp(jax.random.uniform(row_key, (SECTIONS, TOKENS, 1), jnp.float32, math.log(0.2), math.log(2.0)))
    col_scale = jnp.exp(jax.random.uniform(col_key, (SECTIONS, 1, D), jnp.float32, 0.0, math.log(3.2)))
    result = noise * row_scale * col_scale * slope[None, None, :]
    return jnp.clip(result, -30.0, 30.0).astype(jnp.bfloat16)


def query_key(key):
    base = jnp.clip(jax.random.normal(jax.random.fold_in(key, 11), (SECTIONS, D, KVW), jnp.float32), -4.0, 4.0) * D ** (-0.5)
    free_query = jnp.clip(jax.random.normal(jax.random.fold_in(key, 12), (SECTIONS, D, HQ), jnp.float32), -4.0, 4.0) * D ** (-0.5)
    query = free_query
    return (jnp.clip(query, -2.0, 2.0).astype(jnp.bfloat16), jnp.clip(base, -1.0, 1.0).astype(jnp.bfloat16))


def draw_x_down(key, part):
    return activations(jax.random.fold_in(key, 3))


def draw_x_up(key, part):
    return activations(jax.random.fold_in(key, 4))


def draw_wq_down(key, part):
    return query_key(jax.random.fold_in(key, 1))[0]


def draw_wk_down(key, part):
    return query_key(jax.random.fold_in(key, 1))[1]


def draw_wq_up(key, part):
    return query_key(jax.random.fold_in(key, 2))[0]


def draw_wk_up(key, part):
    return query_key(jax.random.fold_in(key, 2))[1]


def level_of(own_key, dims, cuts, low, largest):
    def one(axis_at, parts):
        steps = jax.random.uniform(jax.random.fold_in(jax.random.fold_in(own_key, 6), axis_at), (parts,), jnp.float32, low / len(cuts), largest / len(cuts))
        return jnp.repeat(jnp.exp(steps), dims[axis_at] // parts).reshape((-1,) + (1,) * (len(dims) - axis_at - 1))

    level = one(*cuts[0])
    for cut in cuts[1:]:
        level = level * one(*cut)
    return level


def bell_draw(rng, extent, spread, reach, pieces=(), kind=jnp.bfloat16):
    factor_of = level_of(rng, extent, pieces, -0.22, 0.18) if pieces else 1.0
    values = jax.random.normal(rng, extent, jnp.float32) * spread * factor_of
    return jnp.minimum(jnp.maximum(values, -reach), reach).astype(kind)


def setup_inputs(seed: int = 0) -> dict:
    key_list = jax.random.split(jax.random.key(seed), 13)
    x_down = draw_x_down(jax.random.fold_in(key_list[12], 71), 0)
    gain_down = jnp.clip(1.0 + 0.18 * jax.random.normal(key_list[1], (SECTIONS, D), jnp.float32), 0.1, 1.9)
    wq_down = draw_wq_down(jax.random.fold_in(key_list[12], 71), 0)
    wk_down = draw_wk_down(jax.random.fold_in(key_list[12], 71), 0)
    wv_down = bell_draw(key_list[4], (SECTIONS, D, KVW), D ** -0.5, 0.0625, ((0, 8), (1, 4), (2, 8)))
    wo_down = bell_draw(key_list[5], (SECTIONS, HQ, D), HQ ** -0.5, 0.09375, ((0, 8), (1, 8), (2, 4)))
    x_up = draw_x_up(jax.random.fold_in(key_list[12], 71), 0)
    gain_up = jnp.clip(1.0 + 0.18 * jax.random.normal(key_list[7], (SECTIONS, D), jnp.float32), 0.1, 1.9)
    wq_up = draw_wq_up(jax.random.fold_in(key_list[12], 71), 0)
    wk_up = draw_wk_up(jax.random.fold_in(key_list[12], 71), 0)
    wv_up = bell_draw(key_list[10], (SECTIONS, D, KVW), D ** -0.5, 0.0625, ((0, 8), (1, 4), (2, 8)))
    wo_up = bell_draw(key_list[11], (SECTIONS, HQ, D), HQ ** -0.5, 0.09375, ((0, 8), (1, 8), (2, 4)))
    return {"x_down": x_down, "gain_down": gain_down, "wq_down": wq_down, "wk_down": wk_down, "wv_down": wv_down, "wo_down": wo_down, "x_up": x_up, "gain_up": gain_up, "wq_up": wq_up, "wk_up": wk_up, "wv_up": wv_up, "wo_up": wo_up}


epsilon = 1e-05

def rounded(array):
    return lax.optimization_barrier(array.astype(jnp.bfloat16)).astype(jnp.float32)

def rotary(matrix, positions):
    row_count = matrix.shape[0]
    shaped = matrix.reshape(row_count, -1, HD)
    half_width = HD // 2
    inverse = 10000.0 ** (-jnp.arange(half_width, dtype=jnp.float32) / half_width)
    angles = positions[:, None] * inverse[None, :]
    cosine = jnp.cos(angles)[:, None, :]
    sine_part = jnp.sin(angles)[:, None, :]
    front_half = shaped[..., :half_width]
    back_half = shaped[..., half_width:]
    turned = jnp.concatenate([front_half * cosine - back_half * sine_part, back_half * cosine + front_half * sine_part], axis=-1)
    return turned.reshape(row_count, -1)

def attention_block(activ, gain_vector, w_query, w_key, w_value, w_out):
    floats = activ.astype(jnp.float32)
    total_sq = lax.optimization_barrier(jnp.sum(floats * floats, axis=1))
    normed = (floats * lax.rsqrt(total_sq / D + epsilon)[:, None] * gain_vector[None, :]).astype(jnp.bfloat16)
    positions = jnp.arange(TOKENS, dtype=jnp.float32)
    queries = rotary(jnp.dot(normed, w_query, preferred_element_type=jnp.float32), positions)
    keys_all = rotary(jnp.dot(normed, w_key, preferred_element_type=jnp.float32), positions)
    values_all = jnp.dot(normed, w_value, preferred_element_type=jnp.float32)
    group_size = HEADS // KV_HEADS
    query_heads = rounded(queries).reshape(TOKENS, KV_HEADS, group_size, HD)
    key_heads = rounded(keys_all).reshape(TOKENS, KV_HEADS, HD)
    value_heads = rounded(values_all).reshape(TOKENS, KV_HEADS, HD)
    scores = jnp.einsum('qkgd,tkd->kgqt', query_heads, key_heads) * (1.0 / HD ** 0.5)
    visible = positions[:, None] >= positions[None, :]
    masked = jnp.where(visible, scores, -1e+30)
    row_top = lax.optimization_barrier(jnp.max(masked, axis=-1, keepdims=True))
    exponent = jnp.where(visible, jnp.exp(masked - row_top), 0.0)
    row_total = lax.optimization_barrier(jnp.sum(exponent, axis=-1))
    mixed_out = jnp.einsum('kgqt,tkd->kgqd', rounded(exponent), value_heads) / row_total[..., None]
    attended = mixed_out.transpose(2, 0, 1, 3).reshape(TOKENS, HQ).astype(jnp.bfloat16)
    group_width = HQ // N_ROW
    summed = jnp.zeros((TOKENS, D), jnp.float32)
    for group_index in range(N_ROW):
        lower = group_index * group_width
        partial_value = jnp.dot(attended[:, lower:lower + group_width], w_out[lower:lower + group_width], preferred_element_type=jnp.float32)
        summed = summed + rounded(partial_value)
    return (floats + summed).astype(jnp.bfloat16)

def reference(x_down, gain_down, wq_down, wk_down, wv_down, wo_down, x_up, gain_up, wq_up, wk_up, wv_up, wo_up):
    down_list = []
    up_list = []
    for section_index in range(SECTIONS):
        down_list.append(attention_block(x_down[section_index], gain_down[section_index], wq_down[section_index], wk_down[section_index], wv_down[section_index], wo_down[section_index]))
        up_list.append(attention_block(x_up[section_index], gain_up[section_index], wq_up[section_index], wk_up[section_index], wv_up[section_index], wo_up[section_index]))
    next_down = jnp.roll(jnp.stack(down_list), 1, axis=0)
    next_up = jnp.roll(jnp.stack(up_list), -1, axis=0)
    return (next_down, next_up)
```

```python
import functools

import jax
import jax.numpy as jnp
import numpy as np
from jax import lax
from jax.experimental import pallas as pl
from jax.experimental.pallas import tpu as pltpu
from jax.sharding import PartitionSpec as P

D = 8192
HD = 128
BT = 128
MESH = pl.DeviceIdType.MESH
EPS = 1e-05
EXP_FACTOR = float(np.log2(np.e) / np.sqrt(HD))
F32 = jnp.float32
BF16 = jnp.bfloat16


def rope_tables():
    half = HD // 2
    inverse = (10000.0 ** (-np.arange(half, dtype=np.float64) / half)).astype(np.float32)
    angles = (np.arange(1024, dtype=np.float32)[:, None] * inverse[None, :]).astype(np.float32)
    cos = np.cos(angles.astype(np.float64)).astype(np.float32)
    sin = np.sin(angles.astype(np.float64)).astype(np.float32)
    q_cos = np.concatenate([cos, cos], axis=1).reshape(8, BT, HD)
    q_sin = np.concatenate([-sin, sin], axis=1).reshape(8, BT, HD)
    cos_t = cos.reshape(8, BT, half).transpose(0, 2, 1)
    sin_t = sin.reshape(8, BT, half).transpose(0, 2, 1)
    k_cos = np.stack([cos_t[:, :32], cos_t[:, 32:], np.ones_like(cos_t[:, :32])])
    k_sin = np.stack([sin_t[:, :32], sin_t[:, 32:], np.zeros_like(sin_t[:, :32])])
    return q_cos, q_sin, k_cos, k_sin


def kernel(
    x0, g0, wq0, wk0, wv0, wo0, x1, g1, wq1, wk1, wv1, wo1, qc_h, qs_h, kc_h, ks_h,
    out0, out1,
    xr, gr, wq, kvt, wo, xg, ssz, sst, pb, pr, kb, kr, kvg, qf, kt, vt, at, ob, orr, ub,
    qc, qs, kc, ks,
    s_loc, s_tab, s_wsend, s_wrecv, s_xs, s_xr, s_ss, s_sr, s_ps, s_pr, s_ks, s_kr,
    s_gs, s_gr, s_hs, s_hr, s_as, s_ar, s_os, s_or, s_us, s_ur,
):
    sec = lax.axis_index("section")
    row = lax.axis_index("row")
    c = lax.axis_index("col")
    x = lax.div(row, 2)
    k = lax.rem(row, 2)
    nsec = lax.axis_size("section")

    def dx(d):
        return (sec, 2 * lax.rem(x + d + 4, 4) + k, c)

    def dz(d):
        return (sec, row, lax.rem(c + d + 4, 4))

    def ds_(d):
        return (lax.rem(sec + d + nsec, nsec), row, c)

    sib = (sec, 2 * x + (1 - k), c)
    xh = (x0, x1)
    gh = (g0, g1)
    wqh = (wq0, wq1)
    wkh = (wk0, wk1)
    wvh = (wv0, wv1)
    woh = (wo0, wo1)
    outs = (out0, out1)
    pending = []

    def local(src, dst, sem):
        d = pltpu.make_async_copy(src, dst, sem)
        d.start()
        return d

    def remote(src, dst, ssem, rsem, dev):
        d = pltpu.make_async_remote_copy(
            src_ref=src, dst_ref=dst, send_sem=ssem, recv_sem=rsem, device_id=dev,
            device_id_type=MESH,
        )
        d.start()
        pending.append(d)
        return d

    lx = [local(xh[q], xr.at[q], s_loc.at[q, 0]) for q in range(2)]
    lg = [local(gh[q], gr.at[q], s_loc.at[q, 1]) for q in range(2)]

    def load_qkv(q):
        r = [local(wqh[q].at[:, pl.ds(256 * n, 256)], wq.at[q, 2 * k + n], s_loc.at[q, 2 + n])
             for n in range(2)]
        r.append(local(wkh[q], kvt.at[q, 0, k], s_loc.at[q, 4]))
        r.append(local(wvh[q], kvt.at[q, 1, k], s_loc.at[q, 5]))
        return r

    def load_wo(q):
        return [local(woh[q].at[:, pl.ds(512 * n, 512)], wo.at[q, n, k], s_loc.at[q, 6 + n])
                for n in range(4)]

    lw = [load_qkv(0), None]
    tabs = []
    for i in range(4):
        blk = 2 * lax.rem(x - i + 4, 4) + k
        cc = jnp.minimum(c, 2)
        tabs.append(local(qc_h.at[blk], qc.at[i], s_tab.at[0, i]))
        tabs.append(local(qs_h.at[blk], qs.at[i], s_tab.at[1, i]))
        tabs.append(local(kc_h.at[cc, blk], kc.at[i], s_tab.at[2, i]))
        tabs.append(local(ks_h.at[cc, blk], ks.at[i], s_tab.at[3, i]))

    barrier = pltpu.get_barrier_semaphore()
    partners = [dx(1), dx(-1), dx(2), dz(1), dz(-1), dz(2), sib, ds_(1), ds_(-1)]
    for p in partners:
        pl.semaphore_signal(barrier, inc=1, device_id=p, device_id_type=MESH)

    def prepare(q):
        lx[q].wait()
        lg[q].wait()
        for m in range(8):
            rows = pl.ds(16 * m, 16)
            v = xr[q, rows, :].astype(F32)
            xg[q, 0, rows, :] = (v * gr[q]).astype(BF16)
            sq = jnp.sum(v * v, axis=1, keepdims=True)
            ssz_col[m] = jnp.broadcast_to(sq, (16, 128))
        col = jnp.concatenate(ssz_col, axis=0)
        ssz[q, 0] = jnp.transpose(col)[0:8, :]

    ssz_col = [None] * 8

    def gather_start(q):
        a = remote(xg.at[q, 0], xg.at[q, 1], s_xs.at[q, 0], s_xr.at[q, 0], dx(1))
        b = remote(xg.at[q, 0], xg.at[q, 3], s_xs.at[q, 1], s_xr.at[q, 1], dx(-1))
        return a, b

    def gather_forward(q, ab):
        ab[0].wait_recv()
        a = remote(xg.at[q, 1, pl.ds(0, 64)], xg.at[q, 2, pl.ds(0, 64)],
                   s_xs.at[q, 2], s_xr.at[q, 2], dx(1))
        ab[1].wait_recv()
        b = remote(xg.at[q, 3, pl.ds(64, 64)], xg.at[q, 2, pl.ds(64, 64)],
                   s_xs.at[q, 3], s_xr.at[q, 3], dx(-1))
        return a, b

    def squares_z(q):
        return [remote(ssz.at[q, 0], ssz.at[q, d], s_ss.at[q, d - 1], s_sr.at[q, d - 1], dz(d))
                for d in (1, 2, 3)]

    def squares_x(q, sent):
        for d in sent:
            d.wait_recv()
        sst[q, 0] = ssz[q, 0] + ssz[q, 1] + ssz[q, 2] + ssz[q, 3]
        return [remote(sst.at[q, 0], sst.at[q, d], s_ss.at[q, 2 + d], s_sr.at[q, 2 + d], dx(d))
                for d in (1, 2, 3)]

    def swap_qkv(q):
        r = [remote(wqh[q].at[:, pl.ds(256 * n, 256)], wq.at[q, 2 * k + n],
                    s_wsend.at[q, n], s_wrecv.at[q, n], sib) for n in range(2)]
        r.append(remote(wkh[q], kvt.at[q, 0, k], s_wsend.at[q, 2], s_wrecv.at[q, 2], sib))
        r.append(remote(wvh[q], kvt.at[q, 1, k], s_wsend.at[q, 3], s_wrecv.at[q, 3], sib))
        return r

    def swap_wo(q):
        return [remote(woh[q].at[:, pl.ds(512 * n, 512)], wo.at[q, n, k],
                       s_wsend.at[q, 4 + n], s_wrecv.at[q, 4 + n], sib) for n in range(4)]

    def project(q, i):
        y = xg.at[q, i]

        def body(n, carry):
            pb[q, i, n] = jnp.dot(y[...], wq[q, n], preferred_element_type=F32).astype(BF16)
            return carry

        lax.fori_loop(0, 4, body, 0)
        w = kvt[q].reshape(256, 2048)
        kv = lax.dot_general(w, y[...], (((1,), (1,)), ((), ())),
                             preferred_element_type=F32).astype(BF16)
        kb[q, i, 0] = jnp.concatenate([kv[0:32], kv[64:96]], axis=0)
        kb[q, i, 1] = jnp.concatenate([kv[32:64], kv[96:128]], axis=0)
        kb[q, i, 2] = kv[128:192]
        kb[q, i, 3] = kv[192:256]
        r = []
        for d in (1, 2, 3):
            to = lax.rem(c + d, 4)
            r.append(remote(kb.at[q, i, to], kr.at[q, i, d - 1],
                            s_ks.at[q, i, d - 1], s_kr.at[q, i, d - 1], dz(d)))
            r.append(remote(pb.at[q, i, to], pr.at[q, i, d - 1],
                            s_ps.at[q, i, d - 1], s_pr.at[q, i, d - 1], dz(d)))
        return r

    def reduce_block(q, i, sent):
        for d in sent:
            d.wait_recv()
        rs8 = lax.rsqrt(sst[q, i] * (1.0 / D) + EPS)
        rs = rs8[0:1, :]
        a = kb[q, i, c].astype(F32)
        for d in range(3):
            a = a + kr[q, i, d].astype(F32)
        a = a * rs
        top = a[0:32]
        bot = a[32:64]
        kvg[q, k, c, i] = jnp.concatenate(
            [top * kc[i] - bot * ks[i], bot * kc[i] + top * ks[i]], axis=0).astype(BF16)
        col = jnp.transpose(jnp.broadcast_to(rs, (128, 128)))
        for h in range(2):
            lanes = pl.ds(128 * h, 128)
            v = pb[q, i, c, :, lanes].astype(F32)
            for d in range(3):
                v = v + pr[q, i, d, :, lanes].astype(F32)
            v = v * col
            qf[q, i, pl.ds(128 * h, 128), :] = (
                v * qc[i] + pltpu.roll(v, 64, 1) * qs[i]).astype(BF16)

    def kv_send(q):
        r = [remote(kvg.at[q, k, c], kvg.at[q, k, c], s_gs.at[q, d - 1], s_gr.at[q, d - 1], dz(d))
             for d in (1, 2, 3)]
        h = [remote(kvg.at[q, k, c], kvg.at[q, k, c], s_hs.at[q, 0], s_hr.at[q, 0], sib)]
        return r, h

    def kv_forward(q, rh):
        r, h = rh
        for d in (1, 3, 2):
            r[d - 1].wait_recv()
            frm = lax.rem(c - d + 4, 4)
            h.append(remote(kvg.at[q, k, frm], kvg.at[q, k, frm],
                            s_hs.at[q, d], s_hr.at[q, d], sib))
        return h

    def kv_finish(q, h):
        for d in h:
            d.wait_recv()
        for p in range(2):
            for i in range(4):
                lanes = pl.ds(128 * (4 * p + i), 128)
                kt[q, 0:32, lanes] = kvg[q, p, 0, i, 0:32]
                kt[q, 32:64, lanes] = kvg[q, p, 1, i, 0:32]
                kt[q, 64:96, lanes] = kvg[q, p, 0, i, 32:64]
                kt[q, 96:128, lanes] = kvg[q, p, 1, i, 32:64]
                vt[q, 0:64, lanes] = kvg[q, p, 2, i]
                vt[q, 64:128, lanes] = kvg[q, p, 3, i]

    def at_copies(q, i):
        a = pltpu.make_async_remote_copy(
            src_ref=at.at[q, i, c], dst_ref=at.at[q, i, c], send_sem=s_as.at[q, i, 0],
            recv_sem=s_ar.at[q, i, 0], device_id=dz(1), device_id_type=MESH)
        b = pltpu.make_async_remote_copy(
            src_ref=at.at[q, i, c], dst_ref=at.at[q, i, c], send_sem=s_as.at[q, i, 1],
            recv_sem=s_ar.at[q, i, 1], device_id=dz(-1), device_id_type=MESH)
        return a, b

    def attend(q):
        lane = lax.broadcasted_iota(jnp.int32, (1, 128), 1)
        key_pos = jnp.concatenate(
            [lane + 128 * (2 * lax.rem(x - i + 4, 4) + p) for p in range(2) for i in range(4)],
            axis=1)

        def body(t, carry):
            i = lax.rem(t + 1, 4)
            start = 128 * (2 * lax.rem(x - i + 4, 4) + k)
            for h in range(2):
                pos = start + lax.broadcasted_iota(jnp.int32, (128, 1), 0)
                s = jnp.dot(qf[q, i, pl.ds(128 * h, 128), :], kt[q], preferred_element_type=F32)
                s = jnp.where(pos >= key_pos, s, -1e30)
                top = jnp.max(s, axis=1, keepdims=True)
                p = jnp.exp2((s - top) * EXP_FACTOR)
                total = jnp.sum(p, axis=1, keepdims=True)
                o = lax.dot_general(p.astype(BF16), vt[q], (((1,), (1,)), ((), ())),
                                    preferred_element_type=F32)
                at[q, i, c, :, pl.ds(128 * h, 128)] = (o / total).astype(BF16)
            a, b = at_copies(q, i)
            a.start()
            b.start()
            return carry

        lax.fori_loop(0, 4, body, 0)
        for i in range(4):
            pending.extend(at_copies(q, i))

    def at_forward(q, i):
        a, b = at_copies(q, i)
        a.wait_recv()
        prev = lax.rem(c + 3, 4)
        nxt = lax.rem(c + 1, 4)
        e = remote(at.at[q, i, prev, pl.ds(0, 64)], at.at[q, i, prev, pl.ds(0, 64)],
                   s_as.at[q, i, 2], s_ar.at[q, i, 2], dz(1))
        b.wait_recv()
        f = remote(at.at[q, i, nxt, pl.ds(64, 64)], at.at[q, i, nxt, pl.ds(64, 64)],
                   s_as.at[q, i, 3], s_ar.at[q, i, 3], dz(-1))
        return e, f

    def out_copy(q, i, n):
        return pltpu.make_async_remote_copy(
            src_ref=ob.at[q, i, n], dst_ref=orr.at[q, i - 1, n], send_sem=s_os.at[q, i - 1, n],
            recv_sem=s_or.at[q, i - 1, n], device_id=dx(-i), device_id_type=MESH)

    def out_project(q, i, ef):
        for d in ef:
            d.wait_recv()

        def body(n, carry):
            w = wo[q, n].reshape(1024, 512)
            acc = jnp.dot(at[q, i, 0], w[0:256], preferred_element_type=F32)
            for m in range(1, 4):
                acc = acc + jnp.dot(at[q, i, m], w[256 * m:256 * m + 256],
                                    preferred_element_type=F32)
            ob[q, i, n] = acc.astype(BF16)
            if i:
                out_copy(q, i, n).start()
            return carry

        lax.fori_loop(0, 4, body, 0)
        if i:
            for n in range(4):
                pending.append(out_copy(q, i, n))

    def finish(q):
        r = []
        for n in range(4):
            v = xr[q, :, pl.ds(512 * n, 512)].astype(F32) + ob[q, 0, n].astype(F32)
            for i in (1, 2, 3):
                out_copy(q, i, n).wait_recv()
                v = v + orr[q, i - 1, n].astype(F32)
            ub[q, n] = v.astype(BF16)
            r.append(remote(ub.at[q, n], outs[q].at[:, pl.ds(512 * n, 512)],
                            s_us.at[q, n], s_ur.at[q, n], ds_(1 if q == 0 else -1)))
        return r

    prepare(0)
    pl.semaphore_wait(barrier, len(partners))
    ga = gather_start(0)
    za = squares_z(0)
    wa = swap_qkv(0)
    lw[1] = load_qkv(1)
    lo = [load_wo(0), load_wo(1)]
    prepare(1)
    zb = squares_z(1)
    wb = swap_qkv(1)
    for d in lw[0]:
        d.wait()
    for d in wa:
        d.wait_recv()
    pa = [None] * 4
    pa[0] = project(0, 0)
    xa = squares_x(0, za)
    xb = squares_x(1, zb)
    wc = swap_wo(0) + swap_wo(1)
    fa = gather_forward(0, ga)
    gb = gather_start(1)
    pa[1] = project(0, 1)
    pa[3] = project(0, 3)
    for d in lw[1]:
        d.wait()
    for d in wb:
        d.wait_recv()
    pbb = [None] * 4
    for d in fa:
        d.wait_recv()
    pa[2] = project(0, 2)
    for d in tabs:
        d.wait()
    for d in xa + xb:
        d.wait_recv()
    pbb[0] = project(1, 0)
    fb = gather_forward(1, gb)
    for i in (0, 1, 3, 2):
        reduce_block(0, i, pa[i])
    ka = kv_send(0)
    pbb[1] = project(1, 1)
    pbb[3] = project(1, 3)
    ha = kv_forward(0, ka)
    for d in fb:
        d.wait_recv()
    pbb[2] = project(1, 2)
    kv_finish(0, ha)
    attend(0)
    for i in (0, 1, 3, 2):
        reduce_block(1, i, pbb[i])
    kbb = kv_send(1)
    ef = [None] * 4
    for i in (1, 2, 3, 0):
        ef[i] = at_forward(0, i)
    hb = kv_forward(1, kbb)
    kv_finish(1, hb)
    attend(1)
    for d in lo[0] + lo[1]:
        d.wait()
    for d in wc:
        d.wait_recv()
    for i in (1, 2, 3, 0):
        out_project(0, i, ef[i])
    for i in (1, 2, 3, 0):
        ef[i] = at_forward(1, i)
    ra = finish(0)
    for i in (1, 2, 3, 0):
        out_project(1, i, ef[i])
    rb = finish(1)
    for d in ra + rb:
        d.wait_recv()
    for d in pending:
        d.wait_send()


def on_device(
    x_down, gain_down, wq_down, wk_down, wv_down, wo_down, x_up, gain_up, wq_up, wk_up, wv_up, wo_up
):
    tables = [jnp.asarray(t) for t in rope_tables()]
    args = []
    for group in (
        (x_down, gain_down, wq_down, wk_down, wv_down, wo_down),
        (x_up, gain_up, wq_up, wk_up, wv_up, wo_up),
    ):
        xx, gg, q, kk, vv, oo = group
        args += [xx[0], gg, q[0], kk[0].T, vv[0].T, oo[0]]
    dma = pltpu.SemaphoreType.DMA
    vm = pltpu.VMEM
    shape = jax.ShapeDtypeStruct((BT, 2048), BF16)
    out = pl.pallas_call(
        kernel,
        out_shape=(shape, shape),
        in_specs=[pl.BlockSpec(memory_space=pl.ANY)] * 16,
        out_specs=(pl.BlockSpec(memory_space=pl.ANY),) * 2,
        scratch_shapes=[
            vm((2, BT, 2048), BF16),
            vm((2, 1, 2048), F32),
            vm((2, 4, 2048, 256), BF16),
            vm((2, 2, 2, 64, 2048), BF16),
            vm((2, 4, 2, 512, 512), BF16),
            vm((2, 4, BT, 2048), BF16),
            vm((2, 4, 8, 128), F32),
            vm((2, 4, 8, 128), F32),
            vm((2, 4, 4, BT, 256), BF16),
            vm((2, 4, 3, BT, 256), BF16),
            vm((2, 4, 4, 64, BT), BF16),
            vm((2, 4, 3, 64, BT), BF16),
            vm((2, 2, 4, 4, 64, BT), BF16),
            vm((2, 4, 2 * BT, HD), BF16),
            vm((2, HD, 1024), BF16),
            vm((2, HD, 1024), BF16),
            vm((2, 4, 4, BT, 256), BF16),
            vm((2, 4, 4, BT, 512), BF16),
            vm((2, 3, 4, BT, 512), BF16),
            vm((2, 4, BT, 512), BF16),
            vm((4, BT, HD), F32),
            vm((4, BT, HD), F32),
            vm((4, 32, BT), F32),
            vm((4, 32, BT), F32),
            dma((2, 10)),
            dma((4, 4)),
            dma((2, 8)), dma((2, 8)),
            dma((2, 4)), dma((2, 4)),
            dma((2, 6)), dma((2, 6)),
            dma((2, 4, 3)), dma((2, 4, 3)),
            dma((2, 4, 3)), dma((2, 4, 3)),
            dma((2, 3)), dma((2, 3)),
            dma((2, 4)), dma((2, 4)),
            dma((2, 4, 4)), dma((2, 4, 4)),
            dma((2, 3, 4)), dma((2, 3, 4)),
            dma((2, 4)), dma((2, 4)),
        ],
        compiler_params=pltpu.CompilerParams(
            collective_id=0, has_side_effects=True, vmem_limit_bytes=62 << 20),
        name="pair",
    )(*args, *tables)
    return out[0][None], out[1][None]


def solution(mesh):
    in_specs = (
        P("section", "row", "col"),
        P("section", "col"),
        P("section", "col", "row"),
        P("section", "col", "row"),
        P("section", "col", "row"),
        P("section", "row", "col"),
    ) * 2
    out_specs = (P("section", "row", "col"), P("section", "row", "col"))
    return jax.shard_map(
        on_device, mesh=mesh, in_specs=in_specs, out_specs=out_specs, check_vma=False
    )
```

```python
import functools

import jax
import jax.numpy as jnp
import numpy as np
from jax import lax
from jax.experimental import pallas as pl
from jax.experimental.pallas import tpu as pltpu
from jax.sharding import PartitionSpec as P

D = 8192
HD = 128
BT = 128
MESH = pl.DeviceIdType.MESH
EPS = 1e-05
EXP_FACTOR = float(np.log2(np.e) / np.sqrt(HD))
F32 = jnp.float32
BF16 = jnp.bfloat16


def rope_tables():
    half = HD // 2
    inverse = (10000.0 ** (-np.arange(half, dtype=np.float64) / half)).astype(np.float32)
    angles = (np.arange(1024, dtype=np.float32)[:, None] * inverse[None, :]).astype(np.float32)
    cos = np.cos(angles.astype(np.float64)).astype(np.float32)
    sin = np.sin(angles.astype(np.float64)).astype(np.float32)
    q_cos = np.concatenate([cos, cos], axis=1).reshape(8, BT, HD)
    q_sin = np.concatenate([-sin, sin], axis=1).reshape(8, BT, HD)
    cos_t = cos.reshape(8, BT, half).transpose(0, 2, 1)
    sin_t = sin.reshape(8, BT, half).transpose(0, 2, 1)
    k_cos = np.stack([cos_t[:, :32], cos_t[:, 32:], np.ones_like(cos_t[:, :32])])
    k_sin = np.stack([sin_t[:, :32], sin_t[:, 32:], np.zeros_like(sin_t[:, :32])])
    return q_cos, q_sin, k_cos, k_sin


def kernel(
    x0, g0, wq0, wk0, wv0, wo0, x1, g1, wq1, wk1, wv1, wo1, qc_h, qs_h, kc_h, ks_h,
    out0, out1,
    xr, gr, wq, kvt, wo, xg, ssz, sst, pb, rl, sb, pr, kvg, qf, kt, vt, at, ob, ro, so, orr, ub,
    qc, qs, kc, ks,
    s_loc, s_tab, s_wsend, s_wrecv, s_xs, s_xr, s_ss, s_sr, s_ps, s_pr,
    s_gs, s_gr, s_hs, s_hr, s_as, s_ar, s_os, s_or, s_us, s_ur,
):
    sec = lax.axis_index("section")
    row = lax.axis_index("row")
    c = lax.axis_index("col")
    x = lax.div(row, 2)
    k = lax.rem(row, 2)
    nsec = lax.axis_size("section")

    def dx(d):
        return (sec, 2 * lax.rem(x + d + 4, 4) + k, c)

    def dz(d):
        return (sec, row, lax.rem(c + d + 4, 4))

    def ds_(d):
        return (lax.rem(sec + d + nsec, nsec), row, c)

    sib = (sec, 2 * x + (1 - k), c)
    xh = (x0, x1)
    gh = (g0, g1)
    wqh = (wq0, wq1)
    wkh = (wk0, wk1)
    wvh = (wv0, wv1)
    woh = (wo0, wo1)
    outs = (out0, out1)
    pending = []

    def local(src, dst, sem):
        d = pltpu.make_async_copy(src, dst, sem)
        d.start()
        return d

    def remote(src, dst, ssem, rsem, dev):
        d = pltpu.make_async_remote_copy(
            src_ref=src, dst_ref=dst, send_sem=ssem, recv_sem=rsem, device_id=dev,
            device_id_type=MESH,
        )
        d.start()
        pending.append(d)
        return d

    lx = [local(xh[q], xr.at[q], s_loc.at[q, 0]) for q in range(2)]
    lg = [local(gh[q], gr.at[q], s_loc.at[q, 1]) for q in range(2)]

    def load_qkv(q):
        r = [local(wqh[q].at[:, pl.ds(256 * n, 256)], wq.at[q, 2 * k + n], s_loc.at[q, 2 + n])
             for n in range(2)]
        r.append(local(wkh[q], kvt.at[q, 0, k], s_loc.at[q, 4]))
        r.append(local(wvh[q], kvt.at[q, 1, k], s_loc.at[q, 5]))
        return r

    def load_wo(q):
        return [local(woh[q].at[:, pl.ds(512 * n, 512)], wo.at[q, n, k], s_loc.at[q, 6 + n])
                for n in range(4)]

    lw = [load_qkv(0), None]
    tabs = []
    for i in range(4):
        blk = 2 * lax.rem(x - i + 4, 4) + k
        cc = jnp.minimum(c, 2)
        tabs.append(local(qc_h.at[blk], qc.at[i], s_tab.at[0, i]))
        tabs.append(local(qs_h.at[blk], qs.at[i], s_tab.at[1, i]))
        tabs.append(local(kc_h.at[cc, blk], kc.at[i], s_tab.at[2, i]))
        tabs.append(local(ks_h.at[cc, blk], ks.at[i], s_tab.at[3, i]))

    barrier = pltpu.get_barrier_semaphore()
    partners = [dx(1), dx(-1), dx(2), dz(1), dz(-1), dz(2), sib, ds_(1), ds_(-1)]
    for p in partners:
        pl.semaphore_signal(barrier, inc=1, device_id=p, device_id_type=MESH)

    def prepare(q):
        lx[q].wait()
        lg[q].wait()
        for m in range(8):
            rows = pl.ds(16 * m, 16)
            v = xr[q, rows, :].astype(F32)
            xg[q, 0, rows, :] = (v * gr[q]).astype(BF16)
            sq = jnp.sum(v * v, axis=1, keepdims=True)
            ssz_col[m] = jnp.broadcast_to(sq, (16, 128))
        col = jnp.concatenate(ssz_col, axis=0)
        ssz[q, 0] = jnp.transpose(col)[0:8, :]

    ssz_col = [None] * 8

    low = pl.ds(0, 64)
    high = pl.ds(64, 64)

    def gather_start(q):
        own = xg.at[q, 0]
        return [
            remote(own.at[rows], xg.at[q, slot, rows], s_xs.at[q, m], s_xr.at[q, m], dx(d))
            for m, (rows, slot, d) in enumerate(
                ((low, 1, 1), (high, 3, -1), (high, 1, 1), (low, 3, -1)))
        ]

    def gather_forward(q, g):
        g[0].wait_recv()
        a = remote(xg.at[q, 1, low], xg.at[q, 2, low], s_xs.at[q, 4], s_xr.at[q, 4], dx(1))
        g[1].wait_recv()
        b = remote(xg.at[q, 3, high], xg.at[q, 2, high], s_xs.at[q, 5], s_xr.at[q, 5], dx(-1))
        return a, b

    def squares_z(q):
        return [remote(ssz.at[q, 0], ssz.at[q, d], s_ss.at[q, d - 1], s_sr.at[q, d - 1], dz(d))
                for d in (1, 2, 3)]

    def squares_x(q, sent):
        for d in sent:
            d.wait_recv()
        sst[q, 0] = ssz[q, 0] + ssz[q, 1] + ssz[q, 2] + ssz[q, 3]
        return [remote(sst.at[q, 0], sst.at[q, d], s_ss.at[q, 2 + d], s_sr.at[q, 2 + d], dx(d))
                for d in (1, 2, 3)]

    def swap_qkv(q):
        r = [remote(wqh[q].at[:, pl.ds(256 * n, 256)], wq.at[q, 2 * k + n],
                    s_wsend.at[q, n], s_wrecv.at[q, n], sib) for n in range(2)]
        r.append(remote(wkh[q], kvt.at[q, 0, k], s_wsend.at[q, 2], s_wrecv.at[q, 2], sib))
        r.append(remote(wvh[q], kvt.at[q, 1, k], s_wsend.at[q, 3], s_wrecv.at[q, 3], sib))
        return r

    def swap_wo(q):
        return [remote(woh[q].at[:, pl.ds(512 * n, 512)], wo.at[q, n, k],
                       s_wsend.at[q, 4 + n], s_wrecv.at[q, 4 + n], sib) for n in range(4)]

    def project_quarters(q, i, first, count):
        def body(m, carry):
            n = lax.rem(first + m, 4)
            r = jnp.dot(xg[q, i], wq[q, n], preferred_element_type=F32).astype(BF16)
            pb[q, i, n, 0, 0:64] = r[0:64]
            pb[q, i, n, 1, 0:64] = r[64:128]
            return carry

        lax.fori_loop(0, count, body, 0)

    def project_kv(q, i):
        w = kvt[q].reshape(256, 2048)
        kv = lax.dot_general(w, xg[q, i], (((1,), (1,)), ((), ())),
                             preferred_element_type=F32).astype(BF16)
        for n, (t, b) in enumerate(((0, 64), (32, 96), (128, 160), (192, 224))):
            for h in range(2):
                pb[q, i, n, h, 64:80, 0:128] = kv[t + 16 * h:t + 16 * h + 16]
                pb[q, i, n, h, 64:80, 128:256] = kv[b + 16 * h:b + 16 * h + 16]

    nxt = lax.rem(c + 1, 4)
    prev = lax.rem(c + 3, 4)
    far = lax.rem(c + 2, 4)

    def scatter(q, i):
        return [
            remote(src, dst, s_ps.at[q, i, m], s_pr.at[q, i, m], dz(d))
            for m, (src, dst, d) in enumerate((
                (pb.at[q, i, far, 0], rl.at[q, i, 0], 1),
                (pb.at[q, i, far, 1], rl.at[q, i, 1], -1),
                (pb.at[q, i, nxt, 1], pr.at[q, i, 0, 1], 1),
                (pb.at[q, i, prev, 0], pr.at[q, i, 1, 0], -1),
            ))
        ]

    def project(q, i):
        project_kv(q, i)
        project_quarters(q, i, 0, 4)
        return scatter(q, i)

    def relay(q, i, sent):
        for h, (n, d) in enumerate(((nxt, 1), (prev, -1))):
            sent[h].wait_recv()
            sb[q, i, h] = (pb[q, i, n, h].astype(F32) + rl[q, i, h].astype(F32)).astype(BF16)
            sent.append(remote(sb.at[q, i, h], pr.at[q, i, h, h],
                               s_ps.at[q, i, 4 + h], s_pr.at[q, i, 4 + h], dz(d)))

    def reduce_block(q, i, sent):
        for d in sent[2:]:
            d.wait_recv()
        rs8 = lax.rsqrt(sst[q, i] * (1.0 / D) + EPS)
        rs = rs8[0:1, :]
        col = jnp.transpose(jnp.broadcast_to(rs, (128, 128)))
        for h in range(2):
            v = pb[q, i, c, h].astype(F32) + pr[q, i, 0, h].astype(F32) + pr[q, i, 1, h].astype(F32)
            top = v[64:80, 0:128] * rs
            bot = v[64:80, 128:256] * rs
            kcos = kc[i, 16 * h:16 * h + 16]
            ksin = ks[i, 16 * h:16 * h + 16]
            kvg[q, k, c, i, 16 * h:16 * h + 16] = (top * kcos - bot * ksin).astype(BF16)
            kvg[q, k, c, i, 32 + 16 * h:48 + 16 * h] = (bot * kcos + top * ksin).astype(BF16)
            for m in range(2):
                u = v[0:64, 128 * m:128 * m + 128] * col[64 * h:64 * h + 64]
                qf[q, i, 128 * m + 64 * h:128 * m + 64 * h + 64] = (
                    u * qc[i, 64 * h:64 * h + 64]
                    + pltpu.roll(u, 64, 1) * qs[i, 64 * h:64 * h + 64]).astype(BF16)

    def kv_send(q):
        r = [remote(kvg.at[q, k, c], kvg.at[q, k, c], s_gs.at[q, d - 1], s_gr.at[q, d - 1], dz(d))
             for d in (1, 2, 3)]
        h = [remote(kvg.at[q, k, c], kvg.at[q, k, c], s_hs.at[q, 0], s_hr.at[q, 0], sib)]
        return r, h

    def kv_forward(q, rh):
        r, h = rh
        for d in (1, 3, 2):
            r[d - 1].wait_recv()
            frm = lax.rem(c - d + 4, 4)
            h.append(remote(kvg.at[q, k, frm], kvg.at[q, k, frm],
                            s_hs.at[q, d], s_hr.at[q, d], sib))
        return h

    def kv_finish(q, h):
        for d in h:
            d.wait_recv()
        for p in range(2):
            for i in range(4):
                lanes = pl.ds(128 * (4 * p + i), 128)
                kt[q, 0:32, lanes] = kvg[q, p, 0, i, 0:32]
                kt[q, 32:64, lanes] = kvg[q, p, 1, i, 0:32]
                kt[q, 64:96, lanes] = kvg[q, p, 0, i, 32:64]
                kt[q, 96:128, lanes] = kvg[q, p, 1, i, 32:64]
                vt[q, 0:64, lanes] = kvg[q, p, 2, i]
                vt[q, 64:128, lanes] = kvg[q, p, 3, i]

    def attend(q, i):
        lane = lax.broadcasted_iota(jnp.int32, (1, 128), 1)
        key_pos = jnp.concatenate(
            [lane + 128 * (2 * lax.rem(x - m + 4, 4) + p) for p in range(2) for m in range(4)],
            axis=1)
        start = 128 * (2 * lax.rem(x - i + 4, 4) + k)
        pos = start + lax.broadcasted_iota(jnp.int32, (128, 1), 0)

        def body(h, carry):
            s = jnp.dot(qf[q, i, pl.ds(pl.multiple_of(128 * h, 128), 128), :], kt[q],
                        preferred_element_type=F32)
            s = jnp.where(pos >= key_pos, s, -1e30)
            top = jnp.max(s, axis=1, keepdims=True)
            p = jnp.exp2((s - top) * EXP_FACTOR)
            total = jnp.sum(p, axis=1, keepdims=True)
            o = lax.dot_general(p.astype(BF16), vt[q], (((1,), (1,)), ((), ())),
                                preferred_element_type=F32)
            at[q, i, c, :, pl.ds(pl.multiple_of(128 * h, 128), 128)] = (o / total).astype(BF16)
            return carry

        lax.fori_loop(0, 2, body, 0)
        own = at.at[q, i, c]
        return [remote(own, own, s_as.at[q, i, m], s_ar.at[q, i, m], dz(d))
                for m, d in enumerate((1, -1))]

    def at_forward(q, i, sent):
        sent[0].wait_recv()
        src = at.at[q, i, prev, low]
        sent.append(remote(src, src, s_as.at[q, i, 2], s_ar.at[q, i, 2], dz(1)))
        sent[1].wait_recv()
        src = at.at[q, i, nxt, high]
        sent.append(remote(src, src, s_as.at[q, i, 3], s_ar.at[q, i, 3], dz(-1)))

    def out_copies(q, i, n):
        if i == 2:
            plan = ((0, low, ro.at[q, n, 0], 1), (1, high, ro.at[q, n, 1], -1))
        elif i == 3:
            plan = ((2, high, orr.at[q, n, 0, high], 1),)
        elif i == 1:
            plan = ((3, low, orr.at[q, n, 1, low], -1),)
        else:
            plan = ()
        return [
            pltpu.make_async_remote_copy(
                src_ref=ob.at[q, i, n, rows], dst_ref=dst, send_sem=s_os.at[q, m, n],
                recv_sem=s_or.at[q, m, n], device_id=dx(d), device_id_type=MESH)
            for m, rows, dst, d in plan
        ]

    def out_project(q, i, sent):
        for d in sent[2:]:
            d.wait_recv()

        def body(n, carry):
            w = wo[q, n].reshape(1024, 512)
            acc = jnp.dot(at[q, i, 0], w[0:256], preferred_element_type=F32)
            for m in range(1, 4):
                acc = acc + jnp.dot(at[q, i, m], w[256 * m:256 * m + 256],
                                    preferred_element_type=F32)
            ob[q, i, n] = acc.astype(BF16)
            for d in out_copies(q, i, n):
                d.start()
            return carry

        lax.fori_loop(0, 4, body, 0)
        for n in range(4):
            pending.extend(out_copies(q, i, n))

    def relay_copies(q, n):
        return [
            pltpu.make_async_remote_copy(
                src_ref=so.at[q, n, h], dst_ref=orr.at[q, n, h, rows], send_sem=s_os.at[q, 4 + h, n],
                recv_sem=s_or.at[q, 4 + h, n], device_id=dx(d), device_id_type=MESH)
            for h, (rows, d) in enumerate(((low, 1), (high, -1)))
        ]

    def out_relay(q):
        def body(n, carry):
            for d in out_copies(q, 2, n):
                d.wait_recv()
            so[q, n, 0] = (ob[q, 3, n, 0:64].astype(F32) + ro[q, n, 0].astype(F32)).astype(BF16)
            so[q, n, 1] = (ob[q, 1, n, 64:128].astype(F32) + ro[q, n, 1].astype(F32)).astype(BF16)
            for d in relay_copies(q, n):
                d.start()
            return carry

        lax.fori_loop(0, 4, body, 0)
        for n in range(4):
            pending.extend(relay_copies(q, n))

    def finish(q):
        r = []
        for n in range(4):
            for d in out_copies(q, 3, n) + out_copies(q, 1, n) + relay_copies(q, n):
                d.wait_recv()
            v = xr[q, :, pl.ds(512 * n, 512)].astype(F32) + ob[q, 0, n].astype(F32)
            v = v + orr[q, n, 0].astype(F32) + orr[q, n, 1].astype(F32)
            ub[q, n] = v.astype(BF16)
            r.append(remote(ub.at[q, n], outs[q].at[:, pl.ds(512 * n, 512)],
                            s_us.at[q, n], s_ur.at[q, n], ds_(1 if q == 0 else -1)))
        return r

    def wait_all(copies):
        for d in copies:
            d.wait()

    def wait_in(copies):
        for d in copies:
            d.wait_recv()

    prepare(0)
    pl.semaphore_wait(barrier, len(partners))
    ga = gather_start(0)
    za = squares_z(0)
    wa = swap_qkv(0)
    lw[1] = load_qkv(1)
    lo = [load_wo(0), load_wo(1)]
    prepare(1)
    zb = squares_z(1)
    wb = swap_qkv(1)
    wait_all(lw[0])
    project_quarters(0, 0, 2 * k, 2)
    wait_in(wa)
    project_quarters(0, 0, 2 * (1 - k), 2)
    project_kv(0, 0)
    ra = [scatter(0, 0), None, None, None]
    rb = [None] * 4
    ea = [None] * 4
    eb = [None] * 4
    fa = gather_forward(0, ga)
    xa = squares_x(0, za)
    xb = squares_x(1, zb)
    gb = gather_start(1)
    wait_all(lw[1])
    wait_in(wb)
    rb[0] = project(1, 0)
    wc = swap_wo(0) + swap_wo(1)
    relay(0, 0, ra[0])
    wait_in(ga[2:3])
    ra[1] = project(0, 1)
    wait_in(ga[3:4])
    ra[3] = project(0, 3)
    relay(1, 0, rb[0])
    wait_in(fa)
    ra[2] = project(0, 2)
    relay(0, 1, ra[1])
    relay(0, 3, ra[3])
    fb = gather_forward(1, gb)
    wait_all(tabs)
    wait_in(xa + xb)
    reduce_block(0, 0, ra[0])
    relay(0, 2, ra[2])
    wait_in(gb[2:3])
    rb[1] = project(1, 1)
    reduce_block(0, 1, ra[1])
    reduce_block(0, 3, ra[3])
    reduce_block(0, 2, ra[2])
    ka = kv_send(0)
    wait_in(gb[3:4])
    rb[3] = project(1, 3)
    relay(1, 1, rb[1])
    wait_in(fb)
    rb[2] = project(1, 2)
    relay(1, 3, rb[3])
    ha = kv_forward(0, ka)
    kv_finish(0, ha)
    ea[2] = attend(0, 2)
    relay(1, 2, rb[2])
    ea[1] = attend(0, 1)
    ea[3] = attend(0, 3)
    ea[0] = attend(0, 0)
    at_forward(0, 2, ea[2])
    for i in (0, 1, 3, 2):
        reduce_block(1, i, rb[i])
    kbb = kv_send(1)
    at_forward(0, 1, ea[1])
    at_forward(0, 3, ea[3])
    wait_all(lo[0] + lo[1])
    wait_in(wc)
    out_project(0, 2, ea[2])
    at_forward(0, 0, ea[0])
    out_project(0, 1, ea[1])
    hb = kv_forward(1, kbb)
    kv_finish(1, hb)
    eb[2] = attend(1, 2)
    eb[1] = attend(1, 1)
    out_project(0, 3, ea[3])
    at_forward(1, 2, eb[2])
    eb[3] = attend(1, 3)
    out_relay(0)
    at_forward(1, 1, eb[1])
    eb[0] = attend(1, 0)
    out_project(0, 0, ea[0])
    at_forward(1, 3, eb[3])
    out_project(1, 2, eb[2])
    at_forward(1, 0, eb[0])
    out_project(1, 1, eb[1])
    out_project(1, 3, eb[3])
    ua = finish(0)
    out_relay(1)
    out_project(1, 0, eb[0])
    ub_ = finish(1)
    wait_in(ua + ub_)
    for d in pending:
        d.wait_send()


def deliver(a0, a1, b0, b1, held, s_in, s_out):
    rows = [pl.ds(32 * m, 32) for m in range(4)]
    into = [[pltpu.make_async_copy(src.at[r], held.at[q, r], s_in.at[q, m])
             for m, r in enumerate(rows)] for q, src in enumerate((a0, a1))]
    away = [[pltpu.make_async_copy(held.at[q, r], dst.at[r], s_out.at[q, m])
             for m, r in enumerate(rows)] for q, dst in enumerate((b0, b1))]
    for d in into[0] + into[1]:
        d.start()
    for d, e in zip(into[0] + into[1], away[0] + away[1]):
        d.wait()
        e.start()
    for e in away[0] + away[1]:
        e.wait()


def on_device(
    x_down, gain_down, wq_down, wk_down, wv_down, wo_down, x_up, gain_up, wq_up, wk_up, wv_up, wo_up
):
    tables = [jnp.asarray(t) for t in rope_tables()]
    args = []
    for group in (
        (x_down, gain_down, wq_down, wk_down, wv_down, wo_down),
        (x_up, gain_up, wq_up, wk_up, wv_up, wo_up),
    ):
        xx, gg, q, kk, vv, oo = group
        args += [xx[0], gg, q[0], kk[0].T, vv[0].T, oo[0]]
    dma = pltpu.SemaphoreType.DMA
    vm = pltpu.VMEM
    shape = jax.ShapeDtypeStruct((BT, 2048), BF16)
    out = pl.pallas_call(
        kernel,
        out_shape=(shape, shape),
        in_specs=[pl.BlockSpec(memory_space=pl.ANY)] * 16,
        out_specs=(pl.BlockSpec(memory_space=pl.ANY),) * 2,
        scratch_shapes=[
            vm((2, BT, 2048), BF16),
            vm((2, 1, 2048), F32),
            vm((2, 4, 2048, 256), BF16),
            vm((2, 2, 2, 64, 2048), BF16),
            vm((2, 4, 2, 512, 512), BF16),
            vm((2, 4, BT, 2048), BF16),
            vm((2, 4, 8, 128), F32),
            vm((2, 4, 8, 128), F32),
            vm((2, 4, 4, 2, 80, 256), BF16),
            vm((2, 4, 2, 80, 256), BF16),
            vm((2, 4, 2, 80, 256), BF16),
            vm((2, 4, 2, 2, 80, 256), BF16),
            vm((2, 2, 4, 4, 64, BT), BF16),
            vm((2, 4, 2 * BT, HD), BF16),
            vm((2, HD, 1024), BF16),
            vm((2, HD, 1024), BF16),
            vm((2, 4, 4, BT, 256), BF16),
            vm((2, 4, 4, BT, 512), BF16),
            vm((2, 4, 2, 64, 512), BF16),
            vm((2, 4, 2, 64, 512), BF16),
            vm((2, 4, 2, BT, 512), BF16),
            vm((2, 4, BT, 512), BF16),
            vm((4, BT, HD), F32),
            vm((4, BT, HD), F32),
            vm((4, 32, BT), F32),
            vm((4, 32, BT), F32),
            dma((2, 10)),
            dma((4, 4)),
            dma((2, 8)), dma((2, 8)),
            dma((2, 6)), dma((2, 6)),
            dma((2, 6)), dma((2, 6)),
            dma((2, 4, 6)), dma((2, 4, 6)),
            dma((2, 3)), dma((2, 3)),
            dma((2, 4)), dma((2, 4)),
            dma((2, 4, 4)), dma((2, 4, 4)),
            dma((2, 6, 4)), dma((2, 6, 4)),
            dma((2, 4)), dma((2, 4)),
        ],
        compiler_params=pltpu.CompilerParams(
            collective_id=0, has_side_effects=True, vmem_limit_bytes=62 << 20),
        name="pair",
    )(*args, *tables)
    out = pl.pallas_call(
        deliver,
        out_shape=(shape, shape),
        in_specs=[pl.BlockSpec(memory_space=pl.ANY)] * 2,
        out_specs=(pl.BlockSpec(memory_space=pl.ANY),) * 2,
        scratch_shapes=[vm((2, BT, 2048), BF16), dma((2, 4)), dma((2, 4))],
        name="deliver",
    )(*out)
    return out[0][None], out[1][None]


def solution(mesh):
    in_specs = (
        P("section", "row", "col"),
        P("section", "col"),
        P("section", "col", "row"),
        P("section", "col", "row"),
        P("section", "col", "row"),
        P("section", "row", "col"),
    ) * 2
    out_specs = (P("section", "row", "col"), P("section", "row", "col"))
    return jax.shard_map(
        on_device, mesh=mesh, in_specs=in_specs, out_specs=out_specs, check_vma=False
    )
```

```python
import functools

import jax
import jax.numpy as jnp
import numpy as np
from jax import lax
from jax.experimental import pallas as pl
from jax.experimental.pallas import tpu as pltpu
from jax.sharding import PartitionSpec as P

D = 8192
HD = 128
BT = 128
MESH = pl.DeviceIdType.MESH
EPS = 1e-05
EXP_FACTOR = float(np.log2(np.e) / np.sqrt(HD))
F32 = jnp.float32
BF16 = jnp.bfloat16


def rope_tables():
    half = HD // 2
    inverse = (10000.0 ** (-np.arange(half, dtype=np.float64) / half)).astype(np.float32)
    angles = (np.arange(1024, dtype=np.float32)[:, None] * inverse[None, :]).astype(np.float32)
    cos = np.cos(angles.astype(np.float64)).astype(np.float32)
    sin = np.sin(angles.astype(np.float64)).astype(np.float32)
    q_cos = np.concatenate([cos, cos], axis=1).reshape(8, BT, HD)
    q_sin = np.concatenate([-sin, sin], axis=1).reshape(8, BT, HD)
    cos_t = cos.reshape(8, BT, half).transpose(0, 2, 1)
    sin_t = sin.reshape(8, BT, half).transpose(0, 2, 1)
    k_cos = np.stack([cos_t[:, :32], cos_t[:, 32:], np.ones_like(cos_t[:, :32])])
    k_sin = np.stack([sin_t[:, :32], sin_t[:, 32:], np.zeros_like(sin_t[:, :32])])
    return np.stack([q_cos, q_sin], axis=1), np.stack([k_cos, k_sin], axis=2)


def kernel(
    x0, g0, wq0, wk0, wv0, wo0, x1, g1, wq1, wk1, wv1, wo1, qt_h, kt_h,
    out0, out1,
    xr, gr, wq, kvt, wo, xg, ssz, sst, pb, rl, sb, pr, kvg, qf, kt, vt, at, ob, ro, so, orr, ub,
    qt, ktab,
    s_loc, s_tab, s_wq, s_kvw, s_wo, s_xr, s_sr, s_pr, s_gr, s_hr, s_ar, s_or, s_ur, s_send,
):
    sec = lax.axis_index("section")
    row = lax.axis_index("row")
    c = lax.axis_index("col")
    x = lax.div(row, 2)
    k = lax.rem(row, 2)
    nsec = lax.axis_size("section")

    def dx(d):
        return (sec, 2 * lax.rem(x + d + 4, 4) + k, c)

    def dz(d):
        return (sec, row, lax.rem(c + d + 4, 4))

    def ds_(d):
        return (lax.rem(sec + d + nsec, nsec), row, c)

    sib = (sec, 2 * x + (1 - k), c)
    xh = (x0, x1)
    gh = (g0, g1)
    wqh = (wq0, wq1)
    wkh = (wk0, wk1)
    wvh = (wv0, wv1)
    woh = (wo0, wo1)
    outs = (out0, out1)
    two = pl.ds(0, 2)
    three = pl.ds(0, 3)
    sent_bytes = (
        xg.at[two, three], ssz.at[two, three], sst.at[two, three], kvt.at[two, 0],
        wq.at[two, two], wo.at[two, two], pb.at[two, three], kvg.at[two, 0, three],
        kvg.at[two, 0], at.at[two, three], ob.at[two, three], ub,
    )

    def await_bytes(ref, sem):
        pltpu.make_async_copy(ref, ref, sem).wait()

    def local(src, dst, sem):
        d = pltpu.make_async_copy(src, dst, sem)
        d.start()
        return d

    def message(src, dst, kind, rsem, dev):
        return pltpu.make_async_remote_copy(
            src_ref=src, dst_ref=dst, send_sem=s_send.at[kind], recv_sem=rsem, device_id=dev,
            device_id_type=MESH,
        )

    def remote(src, dst, kind, rsem, dev):
        message(src, dst, kind, rsem, dev).start()

    lx = [local(xh[q], xr.at[q], s_loc.at[q, 0]) for q in range(2)]
    lg = [local(gh[q], gr.at[q], s_loc.at[q, 1]) for q in range(2)]

    def load_qkv(q):
        local(wkh[q], kvt.at[q, 0, k], s_kvw.at[q])
        local(wvh[q], kvt.at[q, 1, k], s_kvw.at[q])
        for n in range(2):
            local(wqh[q].at[:, pl.ds(256 * n, 256)], wq.at[q, 2 * k + n], s_wq.at[q, 2 * k + n])

    def load_wo(q):
        for n in range(4):
            local(woh[q].at[:, pl.ds(512 * n, 512)], wo.at[q, n, k], s_wo.at[q])

    load_qkv(0)
    for i in range(4):
        blk = 2 * lax.rem(x - i + 4, 4) + k
        local(qt_h.at[blk], qt.at[i], s_tab.at[0])
        local(kt_h.at[jnp.minimum(c, 2), blk], ktab.at[i], s_tab.at[1])

    barrier = pltpu.get_barrier_semaphore()
    partners = [dx(1), dx(-1), dx(2), dz(1), dz(-1), dz(2), sib, ds_(1), ds_(-1)]
    for p in partners:
        pl.semaphore_signal(barrier, inc=1, device_id=p, device_id_type=MESH)

    def prepare(q):
        lx[q].wait()
        lg[q].wait()
        for m in range(8):
            rows = pl.ds(16 * m, 16)
            v = xr[q, rows, :].astype(F32)
            xg[q, 0, rows, :] = (v * gr[q]).astype(BF16)
            sq = jnp.sum(v * v, axis=1, keepdims=True)
            ssz_col[m] = jnp.broadcast_to(sq, (16, 128))
        col = jnp.concatenate(ssz_col, axis=0)
        ssz[q, 0] = jnp.transpose(col)[0:8, :]

    ssz_col = [None] * 8

    low = pl.ds(0, 64)
    high = pl.ds(64, 64)

    def gather_start(q):
        own = xg.at[q, 0]
        for m, (rows, slot, d) in enumerate(
                ((low, 1, 1), (high, 3, -1), (high, 1, 1), (low, 3, -1))):
            remote(own.at[rows], xg.at[q, slot, rows], 0, s_xr.at[q, m], dx(d))

    def gather_wait(q, m):
        slot, rows = ((1, low), (3, high), (1, high), (3, low))[m]
        await_bytes(xg.at[q, slot, rows], s_xr.at[q, m])

    def gather_forward(q):
        gather_wait(q, 0)
        remote(xg.at[q, 1, low], xg.at[q, 2, low], 0, s_xr.at[q, 4], dx(1))
        gather_wait(q, 1)
        remote(xg.at[q, 3, high], xg.at[q, 2, high], 0, s_xr.at[q, 4], dx(-1))

    def gather_last(q):
        await_bytes(xg.at[q, 2], s_xr.at[q, 4])

    others = pl.ds(1, 3)

    def squares_z(q):
        for d in (1, 2, 3):
            remote(ssz.at[q, 0], ssz.at[q, d], 1, s_sr.at[q, 0], dz(d))

    def squares_x(q):
        await_bytes(ssz.at[q, others], s_sr.at[q, 0])
        sst[q, 0] = ssz[q, 0] + ssz[q, 1] + ssz[q, 2] + ssz[q, 3]
        for d in (1, 2, 3):
            remote(sst.at[q, 0], sst.at[q, d], 2, s_sr.at[q, 1], dx(d))

    def squares_done(q):
        await_bytes(sst.at[q, others], s_sr.at[q, 1])

    def swap_qkv(q):
        remote(wkh[q], kvt.at[q, 0, k], 3, s_kvw.at[q], sib)
        remote(wvh[q], kvt.at[q, 1, k], 3, s_kvw.at[q], sib)
        for n in range(2):
            remote(wqh[q].at[:, pl.ds(256 * n, 256)], wq.at[q, 2 * k + n], 4,
                   s_wq.at[q, 2 * k + n], sib)

    def swap_wo(q):
        for n in range(4):
            remote(woh[q].at[:, pl.ds(512 * n, 512)], wo.at[q, n, k], 5, s_wo.at[q], sib)

    def quarter_ready(q, n):
        await_bytes(wq.at[q, n], s_wq.at[q, n])

    def project_quarters(q, i, first, count, arrive=False):
        def body(m, carry):
            n = lax.rem(first + m, 4)
            if arrive:
                quarter_ready(q, n)
            r = jnp.dot(xg[q, i], wq[q, n], preferred_element_type=F32).astype(BF16)
            pb[q, i, n, 0, 0:64] = r[0:64]
            pb[q, i, n, 1, 0:64] = r[64:128]
            return carry

        lax.fori_loop(0, count, body, 0)

    def project_kv(q, i):
        w = kvt[q].reshape(256, 2048)
        kv = lax.dot_general(w, xg[q, i], (((1,), (1,)), ((), ())),
                             preferred_element_type=F32).astype(BF16)
        for n, (t, b) in enumerate(((0, 64), (32, 96), (128, 160), (192, 224))):
            for h in range(2):
                pb[q, i, n, h, 64:80, 0:128] = kv[t + 16 * h:t + 16 * h + 16]
                pb[q, i, n, h, 64:80, 128:256] = kv[b + 16 * h:b + 16 * h + 16]

    nxt = lax.rem(c + 1, 4)
    prev = lax.rem(c + 3, 4)
    far = lax.rem(c + 2, 4)

    def scatter_far(q, i):
        remote(pb.at[q, i, far, 0], rl.at[q, i, 0], 6, s_pr.at[q, i, 0], dz(1))
        remote(pb.at[q, i, far, 1], rl.at[q, i, 1], 6, s_pr.at[q, i, 0], dz(-1))

    def scatter_near(q, i):
        remote(pb.at[q, i, nxt, 1], pr.at[q, i, 0, 1], 6, s_pr.at[q, i, 1], dz(1))
        remote(pb.at[q, i, prev, 0], pr.at[q, i, 1, 0], 6, s_pr.at[q, i, 1], dz(-1))

    def project(q, i, arrive=False):
        project_kv(q, i)
        if arrive:
            project_quarters(q, i, far, 1, True)
            scatter_far(q, i)
            project_quarters(q, i, far + 1, 3, True)
        else:
            project_quarters(q, i, 0, 4)
            scatter_far(q, i)
        scatter_near(q, i)

    def relay(q, i):
        await_bytes(rl.at[q, i], s_pr.at[q, i, 0])
        for h, (n, d) in enumerate(((nxt, 1), (prev, -1))):
            sb[q, i, h] = (pb[q, i, n, h].astype(F32) + rl[q, i, h].astype(F32)).astype(BF16)
            remote(sb.at[q, i, h], pr.at[q, i, h, h], 6, s_pr.at[q, i, 1], dz(d))

    def reduce_send(q, i):
        await_bytes(pr.at[q, i], s_pr.at[q, i, 1])
        rs8 = lax.rsqrt(sst[q, i] * (1.0 / D) + EPS)
        rs = rs8[0:1, :]
        col = jnp.transpose(jnp.broadcast_to(rs, (128, 128)))
        for h in range(2):
            v = pb[q, i, c, h].astype(F32) + pr[q, i, 0, h].astype(F32) + pr[q, i, 1, h].astype(F32)
            top = v[64:80, 0:128] * rs
            bot = v[64:80, 128:256] * rs
            kcos = ktab[i, 0, 16 * h:16 * h + 16]
            ksin = ktab[i, 1, 16 * h:16 * h + 16]
            kvg[q, k, c, i, 16 * h:16 * h + 16] = (top * kcos - bot * ksin).astype(BF16)
            kvg[q, k, c, i, 32 + 16 * h:48 + 16 * h] = (bot * kcos + top * ksin).astype(BF16)
            for m in range(2):
                u = v[0:64, 128 * m:128 * m + 128] * col[64 * h:64 * h + 64]
                qf[q, i, 128 * m + 64 * h:128 * m + 64 * h + 64] = (
                    u * qt[i, 0, 64 * h:64 * h + 64]
                    + pltpu.roll(u, 64, 1) * qt[i, 1, 64 * h:64 * h + 64]).astype(BF16)
        own = kvg.at[q, k, c, i]
        for d in (1, 2, 3):
            remote(own, own, 7, s_gr.at[q, d - 1], dz(d))

    def kv_share(q):
        own = kvg.at[q, k, c]
        remote(own, own, 8, s_hr.at[q], sib)

    def kv_forward(q):
        for d in (1, 3, 2):
            got = kvg.at[q, k, lax.rem(c - d + 4, 4)]
            await_bytes(got, s_gr.at[q, d - 1])
            remote(got, got, 8, s_hr.at[q], sib)

    def kv_finish(q):
        await_bytes(kvg.at[q, 1 - k], s_hr.at[q])
        for p in range(2):
            for i in range(4):
                lanes = pl.ds(128 * (4 * p + i), 128)
                kt[q, 0:32, lanes] = kvg[q, p, 0, i, 0:32]
                kt[q, 32:64, lanes] = kvg[q, p, 1, i, 0:32]
                kt[q, 64:96, lanes] = kvg[q, p, 0, i, 32:64]
                kt[q, 96:128, lanes] = kvg[q, p, 1, i, 32:64]
                vt[q, 0:64, lanes] = kvg[q, p, 2, i]
                vt[q, 64:128, lanes] = kvg[q, p, 3, i]

    def attend(q, i):
        lane = lax.broadcasted_iota(jnp.int32, (1, 128), 1)
        key_pos = jnp.concatenate(
            [lane + 128 * (2 * lax.rem(x - m + 4, 4) + p) for p in range(2) for m in range(4)],
            axis=1)
        start = 128 * (2 * lax.rem(x - i + 4, 4) + k)
        pos = start + lax.broadcasted_iota(jnp.int32, (128, 1), 0)

        def body(h, carry):
            s = jnp.dot(qf[q, i, pl.ds(pl.multiple_of(128 * h, 128), 128), :], kt[q],
                        preferred_element_type=F32)
            s = jnp.where(pos >= key_pos, s, -1e30)
            top = jnp.max(s, axis=1, keepdims=True)
            p = jnp.exp2((s - top) * EXP_FACTOR)
            total = jnp.sum(p, axis=1, keepdims=True)
            o = lax.dot_general(p.astype(BF16), vt[q], (((1,), (1,)), ((), ())),
                                preferred_element_type=F32)
            at[q, i, c, :, pl.ds(pl.multiple_of(128 * h, 128), 128)] = (o / total).astype(BF16)
            return carry

        lax.fori_loop(0, 2, body, 0)
        own = at.at[q, i, c]
        remote(own, own, 9, s_ar.at[q, i, 0], dz(1))
        remote(own, own, 9, s_ar.at[q, i, 1], dz(-1))

    def at_forward(q, i):
        await_bytes(at.at[q, i, prev], s_ar.at[q, i, 0])
        src = at.at[q, i, prev, low]
        remote(src, src, 9, s_ar.at[q, i, 2], dz(1))
        await_bytes(at.at[q, i, nxt], s_ar.at[q, i, 1])
        src = at.at[q, i, nxt, high]
        remote(src, src, 9, s_ar.at[q, i, 2], dz(-1))

    def out_send(q, i, n):
        src = ob.at[q, i, n]
        if i == 2:
            remote(src.at[low], ro.at[q, n, 0], 10, s_or.at[q, n, 0], dx(1))
            remote(src.at[high], ro.at[q, n, 1], 10, s_or.at[q, n, 0], dx(-1))
        elif i == 3:
            remote(src.at[high], orr.at[q, n, 0, high], 10, s_or.at[q, n, 1], dx(1))
        elif i == 1:
            remote(src.at[low], orr.at[q, n, 1, low], 10, s_or.at[q, n, 1], dx(-1))

    def out_project(q, i):
        await_bytes(at.at[q, i, far], s_ar.at[q, i, 2])

        def body(n, carry):
            w = wo[q, n].reshape(1024, 512)
            acc = jnp.dot(at[q, i, 0], w[0:256], preferred_element_type=F32)
            for m in range(1, 4):
                acc = acc + jnp.dot(at[q, i, m], w[256 * m:256 * m + 256],
                                    preferred_element_type=F32)
            ob[q, i, n] = acc.astype(BF16)
            out_send(q, i, n)
            if i == 3:
                await_bytes(ro.at[q, n], s_or.at[q, n, 0])
                so[q, n, 0] = (ob[q, 3, n, 0:64].astype(F32) + ro[q, n, 0].astype(F32)).astype(BF16)
                so[q, n, 1] = (ob[q, 1, n, 64:128].astype(F32) + ro[q, n, 1].astype(F32)).astype(BF16)
                remote(so.at[q, n, 0], orr.at[q, n, 0, low], 10, s_or.at[q, n, 1], dx(1))
                remote(so.at[q, n, 1], orr.at[q, n, 1, high], 10, s_or.at[q, n, 1], dx(-1))
            return carry

        lax.fori_loop(0, 4, body, 0)

    def finish(q):
        for n in range(4):
            await_bytes(orr.at[q, n], s_or.at[q, n, 1])
            v = xr[q, :, pl.ds(512 * n, 512)].astype(F32) + ob[q, 0, n].astype(F32)
            v = v + orr[q, n, 0].astype(F32) + orr[q, n, 1].astype(F32)
            ub[q, n] = v.astype(BF16)
            remote(ub.at[q, n], outs[q].at[:, pl.ds(512 * n, 512)], 11, s_ur.at[q],
                   ds_(1 if q == 0 else -1))

    prepare(0)
    pl.semaphore_wait(barrier, len(partners))
    gather_start(0)
    squares_z(0)
    swap_qkv(0)
    load_qkv(1)
    load_wo(0)
    load_wo(1)
    prepare(1)
    squares_z(1)
    swap_qkv(1)
    await_bytes(kvt.at[0], s_kvw.at[0])
    project(0, 0, True)
    gather_forward(0)
    squares_x(0)
    squares_x(1)
    gather_start(1)
    await_bytes(kvt.at[1], s_kvw.at[1])
    project(1, 0, True)
    swap_wo(0)
    swap_wo(1)
    relay(0, 0)
    gather_wait(0, 2)
    project(0, 1)
    gather_wait(0, 3)
    project(0, 3)
    relay(1, 0)
    gather_last(0)
    project(0, 2)
    relay(0, 1)
    relay(0, 3)
    gather_forward(1)
    await_bytes(qt, s_tab.at[0])
    await_bytes(ktab, s_tab.at[1])
    squares_done(0)
    squares_done(1)
    reduce_send(0, 0)
    relay(0, 2)
    gather_wait(1, 2)
    project(1, 1)
    reduce_send(0, 1)
    reduce_send(0, 3)
    reduce_send(0, 2)
    kv_share(0)
    gather_wait(1, 3)
    project(1, 3)
    gather_last(1)
    project(1, 2)
    kv_forward(0)
    relay(1, 1)
    kv_finish(0)
    attend(0, 2)
    relay(1, 3)
    attend(0, 1)
    relay(1, 2)
    attend(0, 3)
    reduce_send(1, 0)
    at_forward(0, 2)
    reduce_send(1, 1)
    attend(0, 0)
    reduce_send(1, 3)
    at_forward(0, 1)
    reduce_send(1, 2)
    kv_share(1)
    at_forward(0, 3)
    await_bytes(wo.at[0], s_wo.at[0])
    await_bytes(wo.at[1], s_wo.at[1])
    out_project(0, 2)
    out_project(0, 1)
    at_forward(0, 0)
    kv_forward(1)
    out_project(0, 3)
    kv_finish(1)
    attend(1, 2)
    attend(1, 1)
    at_forward(1, 2)
    attend(1, 3)
    at_forward(1, 1)
    attend(1, 0)
    out_project(0, 0)
    out_project(1, 2)
    at_forward(1, 3)
    out_project(1, 1)
    at_forward(1, 0)
    finish(0)
    out_project(1, 3)
    out_project(1, 0)
    finish(1)
    for q in range(2):
        await_bytes(outs[q], s_ur.at[q])
    for n, ref in enumerate(sent_bytes):
        await_bytes(ref, s_send.at[n])


def deliver(a0, a1, b0, b1, held, s_in, s_out):
    rows = [pl.ds(32 * m, 32) for m in range(4)]
    into = [[pltpu.make_async_copy(src.at[r], held.at[q, r], s_in.at[q, m])
             for m, r in enumerate(rows)] for q, src in enumerate((a0, a1))]
    away = [[pltpu.make_async_copy(held.at[q, r], dst.at[r], s_out.at[q, m])
             for m, r in enumerate(rows)] for q, dst in enumerate((b0, b1))]
    for d in into[0] + into[1]:
        d.start()
    for d, e in zip(into[0] + into[1], away[0] + away[1]):
        d.wait()
        e.start()
    for e in away[0] + away[1]:
        e.wait()


def on_device(
    x_down, gain_down, wq_down, wk_down, wv_down, wo_down, x_up, gain_up, wq_up, wk_up, wv_up, wo_up
):
    tables = [jnp.asarray(t) for t in rope_tables()]
    args = []
    for group in (
        (x_down, gain_down, wq_down, wk_down, wv_down, wo_down),
        (x_up, gain_up, wq_up, wk_up, wv_up, wo_up),
    ):
        xx, gg, q, kk, vv, oo = group
        args += [xx[0], gg, q[0], kk[0].T, vv[0].T, oo[0]]
    dma = pltpu.SemaphoreType.DMA
    vm = pltpu.VMEM
    shape = jax.ShapeDtypeStruct((BT, 2048), BF16)
    out = pl.pallas_call(
        kernel,
        out_shape=(shape, shape),
        in_specs=[pl.BlockSpec(memory_space=pl.ANY)] * 14,
        out_specs=(pl.BlockSpec(memory_space=pl.ANY),) * 2,
        scratch_shapes=[
            vm((2, BT, 2048), BF16),
            vm((2, 1, 2048), F32),
            vm((2, 4, 2048, 256), BF16),
            vm((2, 2, 2, 64, 2048), BF16),
            vm((2, 4, 2, 512, 512), BF16),
            vm((2, 4, BT, 2048), BF16),
            vm((2, 4, 8, 128), F32),
            vm((2, 4, 8, 128), F32),
            vm((2, 4, 4, 2, 80, 256), BF16),
            vm((2, 4, 2, 80, 256), BF16),
            vm((2, 4, 2, 80, 256), BF16),
            vm((2, 4, 2, 2, 80, 256), BF16),
            vm((2, 2, 4, 4, 64, BT), BF16),
            vm((2, 4, 2 * BT, HD), BF16),
            vm((2, HD, 1024), BF16),
            vm((2, HD, 1024), BF16),
            vm((2, 4, 4, BT, 256), BF16),
            vm((2, 4, 4, BT, 512), BF16),
            vm((2, 4, 2, 64, 512), BF16),
            vm((2, 4, 2, 64, 512), BF16),
            vm((2, 4, 2, BT, 512), BF16),
            vm((2, 4, BT, 512), BF16),
            vm((4, 2, BT, HD), F32),
            vm((4, 2, 32, BT), F32),
            dma((2, 2)),
            dma((2,)),
            dma((2, 4)),
            dma((2,)),
            dma((2,)),
            dma((2, 5)),
            dma((2, 2)),
            dma((2, 4, 2)),
            dma((2, 3)),
            dma((2,)),
            dma((2, 4, 3)),
            dma((2, 4, 2)),
            dma((2,)),
            dma((12,)),
        ],
        compiler_params=pltpu.CompilerParams(
            collective_id=0, has_side_effects=True, vmem_limit_bytes=62 << 20),
        name="pair",
    )(*args, *tables)
    out = pl.pallas_call(
        deliver,
        out_shape=(shape, shape),
        in_specs=[pl.BlockSpec(memory_space=pl.ANY)] * 2,
        out_specs=(pl.BlockSpec(memory_space=pl.ANY),) * 2,
        scratch_shapes=[vm((2, BT, 2048), BF16), dma((2, 4)), dma((2, 4))],
        name="deliver",
    )(*out)
    return out[0][None], out[1][None]


def solution(mesh):
    in_specs = (
        P("section", "row", "col"),
        P("section", "col"),
        P("section", "col", "row"),
        P("section", "col", "row"),
        P("section", "col", "row"),
        P("section", "row", "col"),
    ) * 2
    out_specs = (P("section", "row", "col"), P("section", "row", "col"))
    return jax.shard_map(
        on_device, mesh=mesh, in_specs=in_specs, out_specs=out_specs, check_vma=False
    )
```

```python
import functools

import jax
import jax.numpy as jnp
import numpy as np
from jax import lax
from jax.experimental import pallas as pl
from jax.experimental.pallas import tpu as pltpu
from jax.sharding import PartitionSpec as P

D = 8192
HD = 128
BT = 128
MESH = pl.DeviceIdType.MESH
EPS = 1e-05
EXP_FACTOR = float(np.log2(np.e) / np.sqrt(HD))
F32 = jnp.float32
BF16 = jnp.bfloat16


def rope_tables():
    half = HD // 2
    inverse = (10000.0 ** (-np.arange(half, dtype=np.float64) / half)).astype(np.float32)
    angles = (np.arange(1024, dtype=np.float32)[:, None] * inverse[None, :]).astype(np.float32)
    cos = np.cos(angles.astype(np.float64)).astype(np.float32)
    sin = np.sin(angles.astype(np.float64)).astype(np.float32)
    q_cos = np.concatenate([cos, cos], axis=1).reshape(8, BT, HD)
    q_sin = np.concatenate([-sin, sin], axis=1).reshape(8, BT, HD)
    cos_t = cos.reshape(8, BT, half).transpose(0, 2, 1)
    sin_t = sin.reshape(8, BT, half).transpose(0, 2, 1)
    k_cos = np.stack([cos_t[:, :32], cos_t[:, 32:], np.ones_like(cos_t[:, :32])])
    k_sin = np.stack([sin_t[:, :32], sin_t[:, 32:], np.zeros_like(sin_t[:, :32])])
    return np.stack([q_cos, q_sin], axis=1), np.stack([k_cos, k_sin], axis=2)


def kernel(
    x0, g0, wq0, wk0, wv0, wo0, x1, g1, wq1, wk1, wv1, wo1, qt_h, kt_h,
    out0, out1,
    xr, gr, wq, kvt, wo, xg, ssz, sst, pb, rl, sb, pr, kvg, qf, kt, vt, at, ob, ro, so, orr, ub,
    qt, ktab,
    s_loc, s_tab, s_wq, s_kvw, s_wo, s_xr, s_sr, s_pr, s_gr, s_hr, s_ar, s_or, s_ur, s_send,
):
    sec = lax.axis_index("section")
    row = lax.axis_index("row")
    c = lax.axis_index("col")
    x = lax.div(row, 2)
    k = lax.rem(row, 2)
    nsec = lax.axis_size("section")

    def dx(d):
        return (sec, 2 * lax.rem(x + d + 4, 4) + k, c)

    def dz(d):
        return (sec, row, lax.rem(c + d + 4, 4))

    def ds_(d):
        return (lax.rem(sec + d + nsec, nsec), row, c)

    sib = (sec, 2 * x + (1 - k), c)
    xh = (x0, x1)
    gh = (g0, g1)
    wqh = (wq0, wq1)
    wkh = (wk0, wk1)
    wvh = (wv0, wv1)
    woh = (wo0, wo1)
    outs = (out0, out1)
    two = pl.ds(0, 2)
    three = pl.ds(0, 3)
    sent_bytes = (
        xg.at[two, three], ssz.at[two, three], sst.at[two, three], kvt.at[two, 0],
        wq.at[two, two], wo.at[two, two], pb.at[two, three], kvg.at[two, 0, three],
        kvg.at[two, 0], at.at[two, two, three], ob.at[two, two, pl.ds(0, 4), three], ub,
    )

    def await_bytes(ref, sem):
        pltpu.make_async_copy(ref, ref, sem).wait()

    def local(src, dst, sem):
        d = pltpu.make_async_copy(src, dst, sem)
        d.start()
        return d

    def message(src, dst, kind, rsem, dev):
        return pltpu.make_async_remote_copy(
            src_ref=src, dst_ref=dst, send_sem=s_send.at[kind], recv_sem=rsem, device_id=dev,
            device_id_type=MESH,
        )

    def remote(src, dst, kind, rsem, dev):
        message(src, dst, kind, rsem, dev).start()

    lx = [local(xh[q], xr.at[q], s_loc.at[q, 0]) for q in range(2)]
    lg = [local(gh[q], gr.at[q], s_loc.at[q, 1]) for q in range(2)]

    def load_qkv(q):
        local(wkh[q], kvt.at[q, 0, k], s_kvw.at[q])
        local(wvh[q], kvt.at[q, 1, k], s_kvw.at[q])
        for n in range(2):
            local(wqh[q].at[:, pl.ds(256 * n, 256)], wq.at[q, 2 * k + n], s_wq.at[q, 2 * k + n])

    def load_wo(q):
        for n in range(4):
            local(woh[q].at[:, pl.ds(512 * n, 512)], wo.at[q, n, k], s_wo.at[q])

    load_qkv(0)
    for i in range(4):
        blk = 2 * lax.rem(x - i + 4, 4) + k
        local(qt_h.at[blk], qt.at[i], s_tab.at[0])
        local(kt_h.at[jnp.minimum(c, 2), blk], ktab.at[i], s_tab.at[1])

    barrier = pltpu.get_barrier_semaphore()
    partners = [dx(1), dx(-1), dx(2), dz(1), dz(-1), dz(2), sib, ds_(1), ds_(-1)]
    for p in partners:
        pl.semaphore_signal(barrier, inc=1, device_id=p, device_id_type=MESH)

    def prepare(q):
        lx[q].wait()
        lg[q].wait()
        for m in range(8):
            rows = pl.ds(16 * m, 16)
            v = xr[q, rows, :].astype(F32)
            xg[q, 0, rows, :] = (v * gr[q]).astype(BF16)
            sq = jnp.sum(v * v, axis=1, keepdims=True)
            ssz_col[m] = jnp.broadcast_to(sq, (16, 128))
        col = jnp.concatenate(ssz_col, axis=0)
        ssz[q, 0] = jnp.transpose(col)[0:8, :]

    ssz_col = [None] * 8

    low = pl.ds(0, 64)
    high = pl.ds(64, 64)

    def gather_start(q):
        own = xg.at[q, 0]
        for m, (rows, slot, d) in enumerate(
                ((low, 1, 1), (high, 3, -1), (high, 1, 1), (low, 3, -1))):
            remote(own.at[rows], xg.at[q, slot, rows], 0, s_xr.at[q, m], dx(d))

    def gather_wait(q, m):
        slot, rows = ((1, low), (3, high), (1, high), (3, low))[m]
        await_bytes(xg.at[q, slot, rows], s_xr.at[q, m])

    def gather_forward(q):
        gather_wait(q, 0)
        remote(xg.at[q, 1, low], xg.at[q, 2, low], 0, s_xr.at[q, 4], dx(1))
        gather_wait(q, 1)
        remote(xg.at[q, 3, high], xg.at[q, 2, high], 0, s_xr.at[q, 4], dx(-1))

    def gather_last(q):
        await_bytes(xg.at[q, 2], s_xr.at[q, 4])

    others = pl.ds(1, 3)

    def squares_z(q):
        for d in (1, 2, 3):
            remote(ssz.at[q, 0], ssz.at[q, d], 1, s_sr.at[q, 0], dz(d))

    def squares_x(q):
        await_bytes(ssz.at[q, others], s_sr.at[q, 0])
        sst[q, 0] = ssz[q, 0] + ssz[q, 1] + ssz[q, 2] + ssz[q, 3]
        for d in (1, 2, 3):
            remote(sst.at[q, 0], sst.at[q, d], 2, s_sr.at[q, 1], dx(d))

    def squares_done(q):
        await_bytes(sst.at[q, others], s_sr.at[q, 1])

    def swap_qkv(q):
        remote(wkh[q], kvt.at[q, 0, k], 3, s_kvw.at[q], sib)
        remote(wvh[q], kvt.at[q, 1, k], 3, s_kvw.at[q], sib)
        for n in range(2):
            remote(wqh[q].at[:, pl.ds(256 * n, 256)], wq.at[q, 2 * k + n], 4,
                   s_wq.at[q, 2 * k + n], sib)

    def swap_wo(q):
        for n in range(4):
            remote(woh[q].at[:, pl.ds(512 * n, 512)], wo.at[q, n, k], 5, s_wo.at[q], sib)

    def quarter_ready(q, n):
        await_bytes(wq.at[q, n], s_wq.at[q, n])

    def project_quarters(q, i, first, count, arrive=False):
        def body(m, carry):
            n = lax.rem(first + m, 4)
            if arrive:
                quarter_ready(q, n)
            r = jnp.dot(xg[q, i], wq[q, n], preferred_element_type=F32).astype(BF16)
            pb[q, i, n, 0, 0:64] = r[0:64]
            pb[q, i, n, 1, 0:64] = r[64:128]
            return carry

        lax.fori_loop(0, count, body, 0)

    def project_kv(q, i):
        w = kvt[q].reshape(256, 2048)
        kv = lax.dot_general(w, xg[q, i], (((1,), (1,)), ((), ())),
                             preferred_element_type=F32).astype(BF16)
        for n, (t, b) in enumerate(((0, 64), (32, 96), (128, 160), (192, 224))):
            for h in range(2):
                pb[q, i, n, h, 64:80, 0:128] = kv[t + 16 * h:t + 16 * h + 16]
                pb[q, i, n, h, 64:80, 128:256] = kv[b + 16 * h:b + 16 * h + 16]

    nxt = lax.rem(c + 1, 4)
    prev = lax.rem(c + 3, 4)
    far = lax.rem(c + 2, 4)

    def scatter_far(q, i):
        remote(pb.at[q, i, far, 0], rl.at[q, i, 0], 6, s_pr.at[q, i, 0], dz(1))
        remote(pb.at[q, i, far, 1], rl.at[q, i, 1], 6, s_pr.at[q, i, 0], dz(-1))

    def scatter_near(q, i):
        remote(pb.at[q, i, nxt, 1], pr.at[q, i, 0, 1], 6, s_pr.at[q, i, 1], dz(1))
        remote(pb.at[q, i, prev, 0], pr.at[q, i, 1, 0], 6, s_pr.at[q, i, 1], dz(-1))

    def project(q, i, arrive=False):
        project_kv(q, i)
        if arrive:
            project_quarters(q, i, far, 1, True)
            scatter_far(q, i)
            project_quarters(q, i, far + 1, 3, True)
        else:
            project_quarters(q, i, 0, 4)
            scatter_far(q, i)
        scatter_near(q, i)

    def relay(q, i):
        await_bytes(rl.at[q, i], s_pr.at[q, i, 0])
        for h, (n, d) in enumerate(((nxt, 1), (prev, -1))):
            sb[q, i, h] = (pb[q, i, n, h].astype(F32) + rl[q, i, h].astype(F32)).astype(BF16)
            remote(sb.at[q, i, h], pr.at[q, i, h, h], 6, s_pr.at[q, i, 1], dz(d))

    def reduce_send(q, i):
        await_bytes(pr.at[q, i], s_pr.at[q, i, 1])
        rs8 = lax.rsqrt(sst[q, i] * (1.0 / D) + EPS)
        rs = rs8[0:1, :]
        col = jnp.transpose(jnp.broadcast_to(rs, (128, 128)))
        for h in range(2):
            v = pb[q, i, c, h].astype(F32) + pr[q, i, 0, h].astype(F32) + pr[q, i, 1, h].astype(F32)
            top = v[64:80, 0:128] * rs
            bot = v[64:80, 128:256] * rs
            kcos = ktab[i, 0, 16 * h:16 * h + 16]
            ksin = ktab[i, 1, 16 * h:16 * h + 16]
            kvg[q, k, c, i, 16 * h:16 * h + 16] = (top * kcos - bot * ksin).astype(BF16)
            kvg[q, k, c, i, 32 + 16 * h:48 + 16 * h] = (bot * kcos + top * ksin).astype(BF16)
            for m in range(2):
                u = v[0:64, 128 * m:128 * m + 128] * col[64 * h:64 * h + 64]
                qf[q, i, h, 64 * m:64 * m + 64] = (
                    u * qt[i, 0, 64 * h:64 * h + 64]
                    + pltpu.roll(u, 64, 1) * qt[i, 1, 64 * h:64 * h + 64]).astype(BF16)
        own = kvg.at[q, k, c, i]
        for d in (1, 2, 3):
            remote(own, own, 7, s_gr.at[q, d - 1], dz(d))

    def kv_share(q):
        own = kvg.at[q, k, c]
        remote(own, own, 8, s_hr.at[q], sib)

    def kv_forward(q):
        for d in (1, 3, 2):
            got = kvg.at[q, k, lax.rem(c - d + 4, 4)]
            await_bytes(got, s_gr.at[q, d - 1])
            remote(got, got, 8, s_hr.at[q], sib)

    def kv_finish(q):
        await_bytes(kvg.at[q, 1 - k], s_hr.at[q])
        for p in range(2):
            for i in range(4):
                lanes = pl.ds(128 * (4 * p + i), 128)
                kt[q, 0:32, lanes] = kvg[q, p, 0, i, 0:32]
                kt[q, 32:64, lanes] = kvg[q, p, 1, i, 0:32]
                kt[q, 64:96, lanes] = kvg[q, p, 0, i, 32:64]
                kt[q, 96:128, lanes] = kvg[q, p, 1, i, 32:64]
                vt[q, 0:64, lanes] = kvg[q, p, 2, i]
                vt[q, 64:128, lanes] = kvg[q, p, 3, i]

    head = pl.ds(0, 32)
    tail = pl.ds(32, 32)

    def attend(q, h, p):
        lane = lax.broadcasted_iota(jnp.int32, (1, 128), 1)
        key_pos = jnp.concatenate(
            [lane + 128 * (2 * lax.rem(x - m + 4, 4) + e) for e in range(2) for m in range(4)],
            axis=1)
        token = lax.broadcasted_iota(jnp.int32, (64, 1), 0)
        token = jnp.concatenate([token, token], axis=0)

        def body(r, carry):
            at_pos = 2 * p + r
            i = 3 - 3 * r if p else 2 - r
            pos = 128 * (2 * lax.rem(x - i + 4, 4) + k) + 64 * h + token
            s = jnp.dot(qf[q, i, h], kt[q], preferred_element_type=F32)
            s = jnp.where(pos >= key_pos, s, -1e30)
            top = jnp.max(s, axis=1, keepdims=True)
            w = jnp.exp2((s - top) * EXP_FACTOR)
            total = jnp.sum(w, axis=1, keepdims=True)
            o = lax.dot_general(w.astype(BF16), vt[q], (((1,), (1,)), ((), ())),
                                preferred_element_type=F32)
            o = (o / total).astype(BF16)
            at[q, h, c, at_pos, :, 0:128] = o[0:64]
            at[q, h, c, at_pos, :, 128:256] = o[64:128]
            own = at.at[q, h, c, at_pos]
            remote(own, own, 9, s_ar.at[q, h, at_pos, 0], dz(1))
            remote(own, own, 9, s_ar.at[q, h, at_pos, 1], dz(-1))
            return carry

        lax.fori_loop(0, 2, body, 0)

    def at_forward(q, h, p):
        for at_pos in (2 * p, 2 * p + 1):
            await_bytes(at.at[q, h, prev, at_pos], s_ar.at[q, h, at_pos, 0])
            src = at.at[q, h, prev, at_pos, head]
            remote(src, src, 9, s_ar.at[q, h, at_pos, 2], dz(1))
            await_bytes(at.at[q, h, nxt, at_pos], s_ar.at[q, h, at_pos, 1])
            src = at.at[q, h, nxt, at_pos, tail]
            remote(src, src, 9, s_ar.at[q, h, at_pos, 2], dz(-1))

    def out_project(q, h, p):
        for at_pos in (2 * p, 2 * p + 1):
            await_bytes(at.at[q, h, far, at_pos], s_ar.at[q, h, at_pos, 2])
        pair = pl.ds(2 * p, 2)

        def body(n, carry):
            w = wo[q, n].reshape(1024, 512)
            acc = jnp.dot(at[q, h, 0, pair].reshape(128, 256), w[0:256],
                          preferred_element_type=F32)
            for m in range(1, 4):
                acc = acc + jnp.dot(at[q, h, m, pair].reshape(128, 256), w[256 * m:256 * m + 256],
                                    preferred_element_type=F32)
            ob[q, h, n, pair] = acc.astype(BF16).reshape(2, 64, 512)
            into, done = s_or.at[q, h, n, 0], s_or.at[q, h, n, 1]
            if p == 0:
                remote(ob.at[q, h, n, 0, head], ro.at[q, h, n, 0], 10, into, dx(1))
                remote(ob.at[q, h, n, 0, tail], ro.at[q, h, n, 1], 10, into, dx(-1))
                remote(ob.at[q, h, n, 1, head], orr.at[q, h, n, 1, head], 10, done, dx(-1))
            else:
                remote(ob.at[q, h, n, 2, tail], orr.at[q, h, n, 0, tail], 10, done, dx(1))
            return carry

        lax.fori_loop(0, 4, body, 0)

    def out_relay(q, h):
        def body(n, carry):
            done = s_or.at[q, h, n, 1]
            await_bytes(ro.at[q, h, n], s_or.at[q, h, n, 0])
            so[q, h, n, 0] = (ob[q, h, n, 2, 0:32].astype(F32)
                              + ro[q, h, n, 0].astype(F32)).astype(BF16)
            so[q, h, n, 1] = (ob[q, h, n, 1, 32:64].astype(F32)
                              + ro[q, h, n, 1].astype(F32)).astype(BF16)
            remote(so.at[q, h, n, 0], orr.at[q, h, n, 0, head], 10, done, dx(1))
            remote(so.at[q, h, n, 1], orr.at[q, h, n, 1, tail], 10, done, dx(-1))
            return carry

        lax.fori_loop(0, 4, body, 0)

    def finish(q, h):
        for n in range(4):
            await_bytes(orr.at[q, h, n], s_or.at[q, h, n, 1])
            v = xr[q, 64 * h:64 * h + 64, 512 * n:512 * n + 512].astype(F32)
            v = v + ob[q, h, n, 3].astype(F32)
            v = v + orr[q, h, n, 0].astype(F32) + orr[q, h, n, 1].astype(F32)
            ub[q, h, n] = v.astype(BF16)
            remote(ub.at[q, h, n], outs[q].at[pl.ds(64 * h, 64), pl.ds(512 * n, 512)], 11,
                   s_ur.at[q], ds_(1 if q == 0 else -1))

    prepare(0)
    pl.semaphore_wait(barrier, len(partners))
    gather_start(0)
    squares_z(0)
    swap_qkv(0)
    load_qkv(1)
    load_wo(0)
    load_wo(1)
    prepare(1)
    squares_z(1)
    swap_qkv(1)
    await_bytes(kvt.at[0], s_kvw.at[0])
    project(0, 0, True)
    gather_forward(0)
    squares_x(0)
    squares_x(1)
    gather_start(1)
    await_bytes(kvt.at[1], s_kvw.at[1])
    project(1, 0, True)
    swap_wo(0)
    swap_wo(1)
    relay(0, 0)
    gather_wait(0, 2)
    project(0, 1)
    gather_wait(0, 3)
    project(0, 3)
    relay(1, 0)
    gather_last(0)
    project(0, 2)
    relay(0, 1)
    relay(0, 3)
    gather_forward(1)
    await_bytes(qt, s_tab.at[0])
    await_bytes(ktab, s_tab.at[1])
    squares_done(0)
    squares_done(1)
    reduce_send(0, 0)
    relay(0, 2)
    gather_wait(1, 2)
    project(1, 1)
    reduce_send(0, 1)
    reduce_send(0, 3)
    reduce_send(0, 2)
    kv_share(0)
    gather_wait(1, 3)
    project(1, 3)
    gather_last(1)
    project(1, 2)
    kv_forward(0)
    relay(1, 1)
    kv_finish(0)
    attend(0, 0, 0)
    relay(1, 3)
    attend(0, 0, 1)
    relay(1, 2)
    attend(0, 1, 0)
    reduce_send(1, 0)
    at_forward(0, 0, 0)
    reduce_send(1, 1)
    attend(0, 1, 1)
    reduce_send(1, 3)
    at_forward(0, 0, 1)
    reduce_send(1, 2)
    kv_share(1)
    at_forward(0, 1, 0)
    await_bytes(wo.at[0], s_wo.at[0])
    await_bytes(wo.at[1], s_wo.at[1])
    out_project(0, 0, 0)
    at_forward(0, 1, 1)
    out_project(0, 0, 1)
    kv_forward(1)
    kv_finish(1)
    attend(1, 0, 0)
    out_relay(0, 0)
    attend(1, 0, 1)
    out_project(0, 1, 0)
    out_project(0, 1, 1)
    at_forward(1, 0, 0)
    attend(1, 1, 0)
    at_forward(1, 0, 1)
    attend(1, 1, 1)
    out_relay(0, 1)
    out_project(1, 0, 0)
    at_forward(1, 1, 0)
    out_project(1, 0, 1)
    at_forward(1, 1, 1)
    finish(0, 0)
    out_relay(1, 0)
    finish(0, 1)
    out_project(1, 1, 0)
    out_project(1, 1, 1)
    finish(1, 0)
    out_relay(1, 1)
    finish(1, 1)
    for q in range(2):
        await_bytes(outs[q], s_ur.at[q])
    for n, ref in enumerate(sent_bytes):
        await_bytes(ref, s_send.at[n])


def deliver(a0, a1, b0, b1, held, s_in, s_out):
    rows = [pl.ds(32 * m, 32) for m in range(4)]
    into = [[pltpu.make_async_copy(src.at[r], held.at[q, r], s_in.at[q, m])
             for m, r in enumerate(rows)] for q, src in enumerate((a0, a1))]
    away = [[pltpu.make_async_copy(held.at[q, r], dst.at[r], s_out.at[q, m])
             for m, r in enumerate(rows)] for q, dst in enumerate((b0, b1))]
    for d in into[0] + into[1]:
        d.start()
    for d, e in zip(into[0] + into[1], away[0] + away[1]):
        d.wait()
        e.start()
    for e in away[0] + away[1]:
        e.wait()


def on_device(
    x_down, gain_down, wq_down, wk_down, wv_down, wo_down, x_up, gain_up, wq_up, wk_up, wv_up, wo_up
):
    tables = [jnp.asarray(t) for t in rope_tables()]
    args = []
    for group in (
        (x_down, gain_down, wq_down, wk_down, wv_down, wo_down),
        (x_up, gain_up, wq_up, wk_up, wv_up, wo_up),
    ):
        xx, gg, q, kk, vv, oo = group
        args += [xx[0], gg, q[0], kk[0].T, vv[0].T, oo[0]]
    dma = pltpu.SemaphoreType.DMA
    vm = pltpu.VMEM
    shape = jax.ShapeDtypeStruct((BT, 2048), BF16)
    out = pl.pallas_call(
        kernel,
        out_shape=(shape, shape),
        in_specs=[pl.BlockSpec(memory_space=pl.ANY)] * 14,
        out_specs=(pl.BlockSpec(memory_space=pl.ANY),) * 2,
        scratch_shapes=[
            vm((2, BT, 2048), BF16),
            vm((2, 1, 2048), F32),
            vm((2, 4, 2048, 256), BF16),
            vm((2, 2, 2, 64, 2048), BF16),
            vm((2, 4, 2, 512, 512), BF16),
            vm((2, 4, BT, 2048), BF16),
            vm((2, 4, 8, 128), F32),
            vm((2, 4, 8, 128), F32),
            vm((2, 4, 4, 2, 80, 256), BF16),
            vm((2, 4, 2, 80, 256), BF16),
            vm((2, 4, 2, 80, 256), BF16),
            vm((2, 4, 2, 2, 80, 256), BF16),
            vm((2, 2, 4, 4, 64, BT), BF16),
            vm((2, 4, 2, BT, HD), BF16),
            vm((2, HD, 1024), BF16),
            vm((2, HD, 1024), BF16),
            vm((2, 2, 4, 4, 64, 256), BF16),
            vm((2, 2, 4, 4, 64, 512), BF16),
            vm((2, 2, 4, 2, 32, 512), BF16),
            vm((2, 2, 4, 2, 32, 512), BF16),
            vm((2, 2, 4, 2, 64, 512), BF16),
            vm((2, 2, 4, 64, 512), BF16),
            vm((4, 2, BT, HD), F32),
            vm((4, 2, 32, BT), F32),
            dma((2, 2)),
            dma((2,)),
            dma((2, 4)),
            dma((2,)),
            dma((2,)),
            dma((2, 5)),
            dma((2, 2)),
            dma((2, 4, 2)),
            dma((2, 3)),
            dma((2,)),
            dma((2, 2, 4, 3)),
            dma((2, 2, 4, 2)),
            dma((2,)),
            dma((12,)),
        ],
        compiler_params=pltpu.CompilerParams(
            collective_id=0, has_side_effects=True, vmem_limit_bytes=62 << 20),
        name="pair",
    )(*args, *tables)
    out = pl.pallas_call(
        deliver,
        out_shape=(shape, shape),
        in_specs=[pl.BlockSpec(memory_space=pl.ANY)] * 2,
        out_specs=(pl.BlockSpec(memory_space=pl.ANY),) * 2,
        scratch_shapes=[vm((2, BT, 2048), BF16), dma((2, 4)), dma((2, 4))],
        name="deliver",
    )(*out)
    return out[0][None], out[1][None]


def solution(mesh):
    in_specs = (
        P("section", "row", "col"),
        P("section", "col"),
        P("section", "col", "row"),
        P("section", "col", "row"),
        P("section", "col", "row"),
        P("section", "row", "col"),
    ) * 2
    out_specs = (P("section", "row", "col"), P("section", "row", "col"))
    return jax.shard_map(
        on_device, mesh=mesh, in_specs=in_specs, out_specs=out_specs, check_vma=False
    )
```

```python
import functools

import jax
import jax.numpy as jnp
import numpy as np
from jax import lax
from jax.experimental import pallas as pl
from jax.experimental.pallas import tpu as pltpu
from jax.sharding import PartitionSpec as P

D = 8192
HD = 128
BT = 128
MESH = pl.DeviceIdType.MESH
EPS = 1e-05
EXP_FACTOR = float(np.log2(np.e) / np.sqrt(HD))
F32 = jnp.float32
BF16 = jnp.bfloat16


def rope_tables():
    half = HD // 2
    inverse = (10000.0 ** (-np.arange(half, dtype=np.float64) / half)).astype(np.float32)
    angles = (np.arange(1024, dtype=np.float32)[:, None] * inverse[None, :]).astype(np.float32)
    cos = np.cos(angles.astype(np.float64)).astype(np.float32)
    sin = np.sin(angles.astype(np.float64)).astype(np.float32)
    q_cos = np.concatenate([cos, cos], axis=1).reshape(8, BT, HD)
    q_sin = np.concatenate([-sin, sin], axis=1).reshape(8, BT, HD)
    cos_t = cos.reshape(8, BT, half).transpose(0, 2, 1)
    sin_t = sin.reshape(8, BT, half).transpose(0, 2, 1)
    k_cos = np.stack([cos_t[:, :32], cos_t[:, 32:], np.ones_like(cos_t[:, :32])])
    k_sin = np.stack([sin_t[:, :32], sin_t[:, 32:], np.zeros_like(sin_t[:, :32])])
    return np.stack([q_cos, q_sin], axis=1), np.stack([k_cos, k_sin], axis=2)


def kernel(
    x0, g0, wq0, wk0, wv0, wo0, x1, g1, wq1, wk1, wv1, wo1, qt_h, kt_h,
    out0, out1,
    xr, gr, wq, kvt, wo, xg, ssz, sst, pb, rl, sb, pr, kvg, qf, kt, vt, at, ob, ro, so, orr, ub,
    qt, ktab,
    s_loc, s_tab, s_wq, s_kvw, s_wo, s_xr, s_sr, s_pr, s_gr, s_hr, s_ar, s_or, s_ur, s_send,
):
    sec = lax.axis_index("section")
    row = lax.axis_index("row")
    c = lax.axis_index("col")
    x = lax.div(row, 2)
    k = lax.rem(row, 2)
    nsec = lax.axis_size("section")

    def dx(d):
        return (sec, 2 * lax.rem(x + d + 4, 4) + k, c)

    def dz(d):
        return (sec, row, lax.rem(c + d + 4, 4))

    def ds_(d):
        return (lax.rem(sec + d + nsec, nsec), row, c)

    sib = (sec, 2 * x + (1 - k), c)
    xh = (x0, x1)
    gh = (g0, g1)
    wqh = (wq0, wq1)
    wkh = (wk0, wk1)
    wvh = (wv0, wv1)
    woh = (wo0, wo1)
    outs = (out0, out1)
    two = pl.ds(0, 2)
    three = pl.ds(0, 3)
    sent_bytes = (
        xg.at[two, three], ssz.at[two, three], sst.at[two, three], kvt.at[two, 0],
        wq.at[two, two], wo.at[two, two], pb.at[two, three], kvg.at[two, 0, three],
        kvg.at[two, 0], at.at[two, two, three], ob.at[two, two, pl.ds(0, 4), three], ub,
    )

    def await_bytes(ref, sem):
        pltpu.make_async_copy(ref, ref, sem).wait()

    def local(src, dst, sem):
        d = pltpu.make_async_copy(src, dst, sem)
        d.start()
        return d

    def message(src, dst, kind, rsem, dev):
        return pltpu.make_async_remote_copy(
            src_ref=src, dst_ref=dst, send_sem=s_send.at[kind], recv_sem=rsem, device_id=dev,
            device_id_type=MESH,
        )

    def remote(src, dst, kind, rsem, dev):
        message(src, dst, kind, rsem, dev).start()

    lx = [local(xh[q], xr.at[q], s_loc.at[q, 0]) for q in range(2)]
    lg = [local(gh[q], gr.at[q], s_loc.at[q, 1]) for q in range(2)]

    def load_qkv(q):
        local(wkh[q], kvt.at[q, 0, k], s_kvw.at[q])
        local(wvh[q], kvt.at[q, 1, k], s_kvw.at[q])
        for n in range(2):
            local(wqh[q].at[:, pl.ds(256 * n, 256)], wq.at[q, 2 * k + n], s_wq.at[q, 2 * k + n])

    def load_wo(q):
        for n in range(4):
            local(woh[q].at[:, pl.ds(512 * n, 512)], wo.at[q, n, k], s_wo.at[q])

    load_qkv(0)
    for i in range(4):
        blk = 2 * lax.rem(x - i + 4, 4) + k
        local(qt_h.at[blk], qt.at[i], s_tab.at[0])
        local(kt_h.at[jnp.minimum(c, 2), blk], ktab.at[i], s_tab.at[1])

    barrier = pltpu.get_barrier_semaphore()
    partners = [dx(1), dx(-1), dx(2), dz(1), dz(-1), dz(2), sib, ds_(1), ds_(-1)]
    for p in partners:
        pl.semaphore_signal(barrier, inc=1, device_id=p, device_id_type=MESH)

    def prepare(q):
        lx[q].wait()
        lg[q].wait()
        for m in range(8):
            rows = pl.ds(16 * m, 16)
            v = xr[q, rows, :].astype(F32)
            xg[q, 0, rows, :] = (v * gr[q]).astype(BF16)
            sq = jnp.sum(v * v, axis=1, keepdims=True)
            ssz_col[m] = jnp.broadcast_to(sq, (16, 128))
        col = jnp.concatenate(ssz_col, axis=0)
        ssz[q, 0] = jnp.transpose(col)[0:8, :]

    ssz_col = [None] * 8

    low = pl.ds(0, 64)
    high = pl.ds(64, 64)

    def gather_start(q):
        own = xg.at[q, 0]
        for m, (rows, slot, d) in enumerate(
                ((low, 1, 1), (high, 3, -1), (high, 1, 1), (low, 3, -1))):
            remote(own.at[rows], xg.at[q, slot, rows], 0, s_xr.at[q, m], dx(d))

    def gather_wait(q, m):
        slot, rows = ((1, low), (3, high), (1, high), (3, low))[m]
        await_bytes(xg.at[q, slot, rows], s_xr.at[q, m])

    def gather_forward(q):
        gather_wait(q, 0)
        remote(xg.at[q, 1, low], xg.at[q, 2, low], 0, s_xr.at[q, 4], dx(1))
        gather_wait(q, 1)
        remote(xg.at[q, 3, high], xg.at[q, 2, high], 0, s_xr.at[q, 4], dx(-1))

    def gather_last(q):
        await_bytes(xg.at[q, 2], s_xr.at[q, 4])

    others = pl.ds(1, 3)

    def squares_z(q):
        for d in (1, 2, 3):
            remote(ssz.at[q, 0], ssz.at[q, d], 1, s_sr.at[q, 0], dz(d))

    def squares_x(q):
        await_bytes(ssz.at[q, others], s_sr.at[q, 0])
        sst[q, 0] = ssz[q, 0] + ssz[q, 1] + ssz[q, 2] + ssz[q, 3]
        for d in (1, 2, 3):
            remote(sst.at[q, 0], sst.at[q, d], 2, s_sr.at[q, 1], dx(d))

    def squares_done(q):
        await_bytes(sst.at[q, others], s_sr.at[q, 1])

    def swap_qkv(q):
        remote(wkh[q], kvt.at[q, 0, k], 3, s_kvw.at[q], sib)
        remote(wvh[q], kvt.at[q, 1, k], 3, s_kvw.at[q], sib)
        for n in range(2):
            remote(wqh[q].at[:, pl.ds(256 * n, 256)], wq.at[q, 2 * k + n], 4,
                   s_wq.at[q, 2 * k + n], sib)

    def swap_wo(q):
        for n in range(4):
            remote(woh[q].at[:, pl.ds(512 * n, 512)], wo.at[q, n, k], 5, s_wo.at[q], sib)

    def quarter_ready(q, n):
        await_bytes(wq.at[q, n], s_wq.at[q, n])

    def project_quarters(q, i, first, count, arrive=False):
        def body(m, carry):
            n = lax.rem(first + m, 4)
            if arrive:
                quarter_ready(q, n)
            r = jnp.dot(xg[q, i], wq[q, n], preferred_element_type=F32).astype(BF16)
            pb[q, i, n, 0, 0:64] = r[0:64]
            pb[q, i, n, 1, 0:64] = r[64:128]
            return carry

        lax.fori_loop(0, count, body, 0)

    def project_kv(q, i):
        w = kvt[q].reshape(256, 2048)
        kv = lax.dot_general(w, xg[q, i], (((1,), (1,)), ((), ())),
                             preferred_element_type=F32).astype(BF16)
        for n, (t, b) in enumerate(((0, 64), (32, 96), (128, 160), (192, 224))):
            for h in range(2):
                pb[q, i, n, h, 64:80, 0:128] = kv[t + 16 * h:t + 16 * h + 16]
                pb[q, i, n, h, 64:80, 128:256] = kv[b + 16 * h:b + 16 * h + 16]

    nxt = lax.rem(c + 1, 4)
    prev = lax.rem(c + 3, 4)
    far = lax.rem(c + 2, 4)

    def scatter_far(q, i):
        remote(pb.at[q, i, far, 0], rl.at[q, i, 0], 6, s_pr.at[q, i, 0], dz(1))
        remote(pb.at[q, i, far, 1], rl.at[q, i, 1], 6, s_pr.at[q, i, 0], dz(-1))

    def scatter_near(q, i):
        remote(pb.at[q, i, nxt, 1], pr.at[q, i, 0, 1], 6, s_pr.at[q, i, 1], dz(1))
        remote(pb.at[q, i, prev, 0], pr.at[q, i, 1, 0], 6, s_pr.at[q, i, 1], dz(-1))

    def project(q, i, arrive=False):
        project_kv(q, i)
        if arrive:
            project_quarters(q, i, far, 1, True)
            scatter_far(q, i)
            project_quarters(q, i, far + 1, 3, True)
        else:
            project_quarters(q, i, 0, 4)
            scatter_far(q, i)
        scatter_near(q, i)

    def relay(q, i):
        await_bytes(rl.at[q, i], s_pr.at[q, i, 0])
        for h, (n, d) in enumerate(((nxt, 1), (prev, -1))):
            sb[q, i, h] = (pb[q, i, n, h].astype(F32) + rl[q, i, h].astype(F32)).astype(BF16)
            remote(sb.at[q, i, h], pr.at[q, i, h, h], 6, s_pr.at[q, i, 1], dz(d))

    def reduce_send(q, i):
        await_bytes(pr.at[q, i], s_pr.at[q, i, 1])
        rs8 = lax.rsqrt(sst[q, i] * (1.0 / D) + EPS)
        rs = rs8[0:1, :]
        col = jnp.transpose(jnp.broadcast_to(rs, (128, 128)))
        for h in range(2):
            v = pb[q, i, c, h].astype(F32) + pr[q, i, 0, h].astype(F32) + pr[q, i, 1, h].astype(F32)
            top = v[64:80, 0:128] * rs
            bot = v[64:80, 128:256] * rs
            kcos = ktab[i, 0, 16 * h:16 * h + 16]
            ksin = ktab[i, 1, 16 * h:16 * h + 16]
            kvg[q, k, c, i, 16 * h:16 * h + 16] = (top * kcos - bot * ksin).astype(BF16)
            kvg[q, k, c, i, 32 + 16 * h:48 + 16 * h] = (bot * kcos + top * ksin).astype(BF16)
            for m in range(2):
                u = v[0:64, 128 * m:128 * m + 128] * col[64 * h:64 * h + 64]
                qf[q, i, h, 64 * m:64 * m + 64] = (
                    u * qt[i, 0, 64 * h:64 * h + 64]
                    + pltpu.roll(u, 64, 1) * qt[i, 1, 64 * h:64 * h + 64]).astype(BF16)
        own = kvg.at[q, k, c, i]
        for d in (1, 2, 3):
            remote(own, own, 7, s_gr.at[q, d - 1], dz(d))

    def kv_share(q):
        own = kvg.at[q, k, c]
        remote(own, own, 8, s_hr.at[q], sib)

    def kv_forward(q):
        for d in (1, 3, 2):
            got = kvg.at[q, k, lax.rem(c - d + 4, 4)]
            await_bytes(got, s_gr.at[q, d - 1])
            remote(got, got, 8, s_hr.at[q], sib)

    def kv_finish(q):
        await_bytes(kvg.at[q, 1 - k], s_hr.at[q])
        for p in range(2):
            for i in range(4):
                lanes = pl.ds(128 * (4 * p + i), 128)
                kt[q, 0:32, lanes] = kvg[q, p, 0, i, 0:32]
                kt[q, 32:64, lanes] = kvg[q, p, 1, i, 0:32]
                kt[q, 64:96, lanes] = kvg[q, p, 0, i, 32:64]
                kt[q, 96:128, lanes] = kvg[q, p, 1, i, 32:64]
                vt[q, 0:64, lanes] = kvg[q, p, 2, i]
                vt[q, 64:128, lanes] = kvg[q, p, 3, i]

    head = pl.ds(0, 32)
    tail = pl.ds(32, 32)

    def attend(q, h, p):
        lane = lax.broadcasted_iota(jnp.int32, (1, 128), 1)
        key_pos = jnp.concatenate(
            [lane + 128 * (2 * lax.rem(x - m + 4, 4) + e) for e in range(2) for m in range(4)],
            axis=1)
        token = lax.broadcasted_iota(jnp.int32, (64, 1), 0)
        token = jnp.concatenate([token, token], axis=0)

        def body(r, carry):
            at_pos = 2 * p + r
            i = 3 - 3 * r if p else 2 - r
            pos = 128 * (2 * lax.rem(x - i + 4, 4) + k) + 64 * h + token
            s = jnp.dot(qf[q, i, h], kt[q], preferred_element_type=F32)
            s = jnp.where(pos >= key_pos, s, -1e30)
            top = jnp.max(s, axis=1, keepdims=True)
            w = jnp.exp2((s - top) * EXP_FACTOR)
            total = jnp.sum(w, axis=1, keepdims=True)
            o = lax.dot_general(w.astype(BF16), vt[q], (((1,), (1,)), ((), ())),
                                preferred_element_type=F32)
            o = (o / total).astype(BF16)
            at[q, h, c, at_pos, :, 0:128] = o[0:64]
            at[q, h, c, at_pos, :, 128:256] = o[64:128]
            own = at.at[q, h, c, at_pos]
            remote(own, own, 9, s_ar.at[q, h, at_pos, 0], dz(1))
            remote(own, own, 9, s_ar.at[q, h, at_pos, 1], dz(-1))
            return carry

        lax.fori_loop(0, 2, body, 0)

    def at_forward(q, h, p):
        for at_pos in (2 * p, 2 * p + 1):
            await_bytes(at.at[q, h, prev, at_pos], s_ar.at[q, h, at_pos, 0])
            src = at.at[q, h, prev, at_pos, head]
            remote(src, src, 9, s_ar.at[q, h, at_pos, 2], dz(1))
            await_bytes(at.at[q, h, nxt, at_pos], s_ar.at[q, h, at_pos, 1])
            src = at.at[q, h, nxt, at_pos, tail]
            remote(src, src, 9, s_ar.at[q, h, at_pos, 2], dz(-1))

    def out_project(q, h, p):
        for at_pos in (2 * p, 2 * p + 1):
            await_bytes(at.at[q, h, far, at_pos], s_ar.at[q, h, at_pos, 2])
        pair = pl.ds(2 * p, 2)

        def body(n, carry):
            w = wo[q, n].reshape(1024, 512)
            acc = jnp.dot(at[q, h, 0, pair].reshape(128, 256), w[0:256],
                          preferred_element_type=F32)
            for m in range(1, 4):
                acc = acc + jnp.dot(at[q, h, m, pair].reshape(128, 256), w[256 * m:256 * m + 256],
                                    preferred_element_type=F32)
            ob[q, h, n, pair] = acc.astype(BF16).reshape(2, 64, 512)
            into, done = s_or.at[q, h, n, 0], s_or.at[q, h, n, 1]
            if p == 0:
                remote(ob.at[q, h, n, 0, head], ro.at[q, h, n, 0], 10, into, dx(1))
                remote(ob.at[q, h, n, 0, tail], ro.at[q, h, n, 1], 10, into, dx(-1))
            else:
                remote(ob.at[q, h, n, 2, tail], orr.at[q, h, n, 0, tail], 10, done, dx(1))
            return carry

        lax.fori_loop(0, 4, body, 0)
        if p == 0:
            for n in range(4):
                remote(ob.at[q, h, n, 1, head], orr.at[q, h, n, 1, head], 10,
                       s_or.at[q, h, n, 1], dx(-1))

    def out_relay(q, h):
        def body(n, carry):
            done = s_or.at[q, h, n, 1]
            await_bytes(ro.at[q, h, n], s_or.at[q, h, n, 0])
            so[q, h, n, 0] = (ob[q, h, n, 2, 0:32].astype(F32)
                              + ro[q, h, n, 0].astype(F32)).astype(BF16)
            so[q, h, n, 1] = (ob[q, h, n, 1, 32:64].astype(F32)
                              + ro[q, h, n, 1].astype(F32)).astype(BF16)
            remote(so.at[q, h, n, 0], orr.at[q, h, n, 0, head], 10, done, dx(1))
            remote(so.at[q, h, n, 1], orr.at[q, h, n, 1, tail], 10, done, dx(-1))
            return carry

        lax.fori_loop(0, 4, body, 0)

    def finish(q, h):
        for n in range(4):
            await_bytes(orr.at[q, h, n], s_or.at[q, h, n, 1])
            v = xr[q, 64 * h:64 * h + 64, 512 * n:512 * n + 512].astype(F32)
            v = v + ob[q, h, n, 3].astype(F32)
            v = v + orr[q, h, n, 0].astype(F32) + orr[q, h, n, 1].astype(F32)
            ub[q, h, n] = v.astype(BF16)
            remote(ub.at[q, h, n], outs[q].at[pl.ds(64 * h, 64), pl.ds(512 * n, 512)], 11,
                   s_ur.at[q], ds_(1 if q == 0 else -1))

    prepare(0)
    pl.semaphore_wait(barrier, len(partners))
    gather_start(0)
    squares_z(0)
    swap_qkv(0)
    load_qkv(1)
    load_wo(0)
    load_wo(1)
    prepare(1)
    squares_z(1)
    swap_qkv(1)
    await_bytes(kvt.at[0], s_kvw.at[0])
    project(0, 0, True)
    gather_forward(0)
    squares_x(0)
    squares_x(1)
    gather_start(1)
    await_bytes(kvt.at[1], s_kvw.at[1])
    project(1, 0, True)
    swap_wo(0)
    swap_wo(1)
    relay(0, 0)
    gather_wait(0, 2)
    project(0, 1)
    gather_wait(0, 3)
    project(0, 3)
    relay(1, 0)
    gather_last(0)
    project(0, 2)
    relay(0, 1)
    relay(0, 3)
    gather_forward(1)
    await_bytes(qt, s_tab.at[0])
    await_bytes(ktab, s_tab.at[1])
    squares_done(0)
    squares_done(1)
    reduce_send(0, 0)
    relay(0, 2)
    gather_wait(1, 2)
    project(1, 1)
    reduce_send(0, 1)
    reduce_send(0, 3)
    reduce_send(0, 2)
    kv_share(0)
    gather_wait(1, 3)
    project(1, 3)
    gather_last(1)
    project(1, 2)
    kv_forward(0)
    relay(1, 1)
    kv_finish(0)
    attend(0, 0, 0)
    relay(1, 3)
    attend(0, 0, 1)
    relay(1, 2)
    attend(0, 1, 0)
    reduce_send(1, 0)
    at_forward(0, 0, 0)
    reduce_send(1, 1)
    attend(0, 1, 1)
    reduce_send(1, 3)
    at_forward(0, 0, 1)
    reduce_send(1, 2)
    kv_share(1)
    at_forward(0, 1, 0)
    await_bytes(wo.at[0], s_wo.at[0])
    await_bytes(wo.at[1], s_wo.at[1])
    out_project(0, 0, 0)
    at_forward(0, 1, 1)
    out_project(0, 0, 1)
    kv_forward(1)
    kv_finish(1)
    attend(1, 0, 0)
    out_relay(0, 0)
    attend(1, 0, 1)
    out_project(0, 1, 0)
    out_project(0, 1, 1)
    at_forward(1, 0, 0)
    attend(1, 1, 0)
    at_forward(1, 0, 1)
    attend(1, 1, 1)
    out_relay(0, 1)
    out_project(1, 0, 0)
    at_forward(1, 1, 0)
    out_project(1, 0, 1)
    at_forward(1, 1, 1)
    finish(0, 0)
    out_relay(1, 0)
    finish(0, 1)
    out_project(1, 1, 0)
    out_project(1, 1, 1)
    finish(1, 0)
    out_relay(1, 1)
    finish(1, 1)
    for q in range(2):
        await_bytes(outs[q], s_ur.at[q])
    for n, ref in enumerate(sent_bytes):
        await_bytes(ref, s_send.at[n])


def deliver(a0, a1, b0, b1, held, s_in, s_out):
    rows = [pl.ds(32 * m, 32) for m in range(4)]
    into = [[pltpu.make_async_copy(src.at[r], held.at[q, r], s_in.at[q, m])
             for m, r in enumerate(rows)] for q, src in enumerate((a0, a1))]
    away = [[pltpu.make_async_copy(held.at[q, r], dst.at[r], s_out.at[q, m])
             for m, r in enumerate(rows)] for q, dst in enumerate((b0, b1))]
    for d in into[0] + into[1]:
        d.start()
    for d, e in zip(into[0] + into[1], away[0] + away[1]):
        d.wait()
        e.start()
    for e in away[0] + away[1]:
        e.wait()


def on_device(
    x_down, gain_down, wq_down, wk_down, wv_down, wo_down, x_up, gain_up, wq_up, wk_up, wv_up, wo_up
):
    tables = [jnp.asarray(t) for t in rope_tables()]
    args = []
    for group in (
        (x_down, gain_down, wq_down, wk_down, wv_down, wo_down),
        (x_up, gain_up, wq_up, wk_up, wv_up, wo_up),
    ):
        xx, gg, q, kk, vv, oo = group
        args += [xx[0], gg, q[0], kk[0].T, vv[0].T, oo[0]]
    dma = pltpu.SemaphoreType.DMA
    vm = pltpu.VMEM
    shape = jax.ShapeDtypeStruct((BT, 2048), BF16)
    out = pl.pallas_call(
        kernel,
        out_shape=(shape, shape),
        in_specs=[pl.BlockSpec(memory_space=pl.ANY)] * 14,
        out_specs=(pl.BlockSpec(memory_space=pl.ANY),) * 2,
        scratch_shapes=[
            vm((2, BT, 2048), BF16),
            vm((2, 1, 2048), F32),
            vm((2, 4, 2048, 256), BF16),
            vm((2, 2, 2, 64, 2048), BF16),
            vm((2, 4, 2, 512, 512), BF16),
            vm((2, 4, BT, 2048), BF16),
            vm((2, 4, 8, 128), F32),
            vm((2, 4, 8, 128), F32),
            vm((2, 4, 4, 2, 80, 256), BF16),
            vm((2, 4, 2, 80, 256), BF16),
            vm((2, 4, 2, 80, 256), BF16),
            vm((2, 4, 2, 2, 80, 256), BF16),
            vm((2, 2, 4, 4, 64, BT), BF16),
            vm((2, 4, 2, BT, HD), BF16),
            vm((2, HD, 1024), BF16),
            vm((2, HD, 1024), BF16),
            vm((2, 2, 4, 4, 64, 256), BF16),
            vm((2, 2, 4, 4, 64, 512), BF16),
            vm((2, 2, 4, 2, 32, 512), BF16),
            vm((2, 2, 4, 2, 32, 512), BF16),
            vm((2, 2, 4, 2, 64, 512), BF16),
            vm((2, 2, 4, 64, 512), BF16),
            vm((4, 2, BT, HD), F32),
            vm((4, 2, 32, BT), F32),
            dma((2, 2)),
            dma((2,)),
            dma((2, 4)),
            dma((2,)),
            dma((2,)),
            dma((2, 5)),
            dma((2, 2)),
            dma((2, 4, 2)),
            dma((2, 3)),
            dma((2,)),
            dma((2, 2, 4, 3)),
            dma((2, 2, 4, 2)),
            dma((2,)),
            dma((12,)),
        ],
        compiler_params=pltpu.CompilerParams(
            collective_id=0, has_side_effects=True, vmem_limit_bytes=62 << 20),
        name="pair",
    )(*args, *tables)
    out = pl.pallas_call(
        deliver,
        out_shape=(shape, shape),
        in_specs=[pl.BlockSpec(memory_space=pl.ANY)] * 2,
        out_specs=(pl.BlockSpec(memory_space=pl.ANY),) * 2,
        scratch_shapes=[vm((2, BT, 2048), BF16), dma((2, 4)), dma((2, 4))],
        name="deliver",
    )(*out)
    return out[0][None], out[1][None]


def solution(mesh):
    in_specs = (
        P("section", "row", "col"),
        P("section", "col"),
        P("section", "col", "row"),
        P("section", "col", "row"),
        P("section", "col", "row"),
        P("section", "row", "col"),
    ) * 2
    out_specs = (P("section", "row", "col"), P("section", "row", "col"))
    return jax.shard_map(
        on_device, mesh=mesh, in_specs=in_specs, out_specs=out_specs, check_vma=False
    )
```
